32 devices in a mesh: group: 2 (over x), expert: 16 (over z, y, core).
Axes of the slice: x: 2, y: 2, z: 4, core: 2. Of those that a mesh axis runs over, the one named last changes fastest.
Arguments:
- hidden: bfloat16 [4096, 4096], P(('group', 'expert')), parts along dimension 0, may hold values from -6 to 6
- norm_gain: bfloat16 [4096], replicated, may hold values from 0.25 to 1.75
- router_weight: bfloat16 [4096, 128], replicated, may hold values from -0.03125 to 0.03125
- expert_ids: int32 [4096, 8], P(('group', 'expert')), parts along dimension 0, may hold values from 0 to 127, all different within a row; in each aligned block of 128 rows (0 to 127, 128 to 255, ...) at most 16 rows name the same one
- gate_weight: bfloat16 [16, 4096, 384], P('expert'), may hold values from -0.09375 to 0.09375
- up_weight: bfloat16 [16, 4096, 384], P('expert'), may hold values from -0.09375 to 0.09375
- down_weight: bfloat16 [16, 384, 4096], P('expert'), may hold values from -0.625 to 0.625
Outputs:
- moe_out: bfloat16 [4096, 4096], P(('group', 'expert')), parts along dimension 0
The draws below stay inside these ranges and needn't reach their ends.
There are 2 independent parts, one for each index of `group`. The reference program is written for one: setup_inputs(seed, part) draws one part's arguments, and reference() takes and returns one part's arrays. A program takes and returns all parts, laid end to end along the dimension named above; an argument that names none is the same for every part. Nothing has to cross between parts.
Inputs may be any that keep to these rules, and one draw needn't show every extreme that they name: `expert_ids`: each row names 8 different experts; in each aligned block of 128 rows (the rows of one device) no expert is named by more than 16 rows.
All inputs are finite; a program needn't handle non-finite values.
Results may differ from the reference program's by a relative error of at most 0.0077.
Values may be sent and summed in bfloat16 or wider, within the bound.
A program may use at most 128 MiB of HBM per device.

```python
import math
import jax
import jax.numpy as jnp
import numpy as np
from jax import lax

D = 4096
FF = 1536
EXPERTS = 128
TOP = 8
TOK_DEV = 128
SPLIT = 4
SLICE = 384
E_FLIGHT = 4
CAP = 16
TOKENS = 2048
N_EXPERT = 16


def levels(stream_key, extent, pieces, least, largest):
    factor_of, own = 1.0, jax.random.fold_in(stream_key, 6)
    for position, blocks in pieces:
        steps = jnp.exp(jax.random.uniform(jax.random.fold_in(own, position), (blocks,), jnp.float32, least / len(pieces), largest / len(pieces)))
        factor_of = factor_of * jnp.repeat(steps, extent[position] // blocks).reshape([-1 if axis == position else 1 for axis in range(len(extent))])
    return factor_of


def shared_out(key, own, number, rows, count, top, reach, lean):
    ranking = jax.random.permutation(key, count)
    packed, usual = load_shares(count, rows * top, reach, lean, True), load_shares(count, rows * top, reach, lean, False)
    places = jnp.arange(count)

    def named(lengths, turn):
        used = int((lengths > 0).sum())
        fixed = max(1, used // 4)
        shifted = fixed + (places - fixed + turn * (used - fixed)) % max(1, count - fixed)
        return jnp.zeros((count,), jnp.int32).at[ranking[jnp.where(places < fixed, places, shifted)]].set(jnp.asarray(lengths, jnp.int32))

    lengths = jnp.where(number % 4 == 0, named(packed, number // 4), named(usual, number - number // 4 - 1))
    mixed = jax.random.permutation(jax.random.fold_in(own, 3), count)
    donor, sink = mixed[0:count // 2 * 2:2], mixed[1:count // 2 * 2:2]
    room = jnp.minimum(lengths[donor] - 1, reach - lengths[sink]) // 2
    room = jnp.where((donor == ranking[0]) | (sink == ranking[0]) | (lengths[sink] == 0), 0, jnp.maximum(room, 0))
    shifted = jax.random.randint(jax.random.fold_in(own, 4), (count // 2,), 0, 1 << 20) % (room + 1)
    lengths = lengths.at[donor].add(-shifted).at[sink].add(shifted)
    labels = jnp.searchsorted(jnp.cumsum(lengths), jnp.arange(rows * top), side="right").astype(jnp.int32)
    table = labels.reshape(top, rows).T
    table = table[jax.random.permutation(jax.random.fold_in(own, 1), rows)]
    turn = jax.random.randint(jax.random.fold_in(own, 2), (rows, 1), 0, top)
    return jnp.take_along_axis(table, (jnp.arange(top)[None, :] + turn) % top, axis=1)


def load_shares(number_of, total, most, skew, full):
    loads = [(1 << 20) // math.isqrt(rank ** skew) + 1 for rank in range(1, number_of + 1)]
    largest = most if full else min(most, max(-(-total // number_of), total * loads[0] // sum(loads)))
    least = 1 if total - largest >= number_of - 1 else 0
    holding, rest = [largest] + [least] * (number_of - 1), total - largest - least * (number_of - 1)
    while rest > 0:
        free = [i for i in range(1, number_of) if holding[i] < largest] or [i for i in range(1, number_of) if holding[i] < most]
        whole, remaining = sum([loads[i] for i in free]), rest
        for i in free:
            more = min(most - holding[i], max(1, remaining * loads[i] // whole), rest)
            holding[i] = holding[i] + more
            rest = rest - more
    return np.array(holding)


def noise(key, dims, width, limit, cuts=(), kind=jnp.bfloat16):
    drawn = jax.random.normal(key, dims, jnp.float32) * width
    if len(cuts) > 0:
        drawn = levels(key, dims, cuts, -0.22, 0.18) * drawn
    return jnp.clip(drawn, min=-limit, max=limit).astype(kind)


def setup_inputs(seed: int = 0, part: int = 0) -> dict:
    keys = jax.random.split(jax.random.key(seed), 8)
    part_splits = jax.random.split(jax.random.fold_in(keys[7], part), 8)
    hidden = noise(part_splits[0], (TOKENS, D), 1.0, 6.0, ((0, 16),))
    norm_gain = jnp.clip(1.0 + 0.15 * jax.random.normal(keys[1], (D,), jnp.float32), 0.25, 1.75).astype(jnp.bfloat16)
    router_weight = noise(keys[2], (D, EXPERTS), (8 * D) ** -0.5, 0.03125)
    expert_ids_keys = jax.random.split(jax.random.fold_in(part_splits[3], 1), TOKENS // TOK_DEV)
    expert_ids_turns = jax.random.permutation(jax.random.fold_in(part_splits[3], 3), TOKENS // TOK_DEV)
    expert_ids = jax.vmap(lambda own, number: shared_out(jax.random.fold_in(part_splits[3], 2), own, number, TOK_DEV, EXPERTS, TOP, CAP, 2))(expert_ids_keys, expert_ids_turns).reshape((TOKENS, TOP))
    gate_weight = noise(keys[4], (N_EXPERT, D, SLICE), D ** -0.5, 0.09375, ((0, 16),))
    up_weight = noise(keys[5], (N_EXPERT, D, SLICE), D ** -0.5, 0.09375, ((0, 16),))
    down_weight = noise(keys[6], (N_EXPERT, SLICE, D), (FF // 16) ** -0.5, 0.625, ((0, 16),))
    return {"hidden": hidden, "norm_gain": norm_gain, "router_weight": router_weight, "expert_ids": expert_ids, "gate_weight": gate_weight, "up_weight": up_weight, "down_weight": down_weight}


def reference(hidden, norm_gain, router_weight, expert_ids, gate_weight, up_weight, down_weight):
    widened = hidden.astype(jnp.float32)
    inv_rms = lax.rsqrt(lax.optimization_barrier(jnp.mean(widened * widened, axis=-1, keepdims=True)) + 1e-06)
    normed = (widened * inv_rms * norm_gain.astype(jnp.float32)).astype(jnp.bfloat16)
    logits = jnp.dot(normed, router_weight, preferred_element_type=jnp.float32)
    router_probs = jax.nn.softmax(logits, axis=-1)
    picked = jnp.take_along_axis(router_probs, expert_ids, axis=1)
    gate_share = picked / lax.optimization_barrier(jnp.sum(picked, axis=1, keepdims=True))

    def one_expert(expert, running):
        summed = jnp.zeros(hidden.shape, jnp.float32)
        for member in range(SPLIT):
            shard_row = member * E_FLIGHT + expert
            gate_mat = lax.dynamic_index_in_dim(gate_weight, shard_row, 0, keepdims=False)
            up_mat = lax.dynamic_index_in_dim(up_weight, shard_row, 0, keepdims=False)
            down_mat = lax.dynamic_index_in_dim(down_weight, shard_row, 0, keepdims=False)
            gate_act = jnp.dot(normed, gate_mat, preferred_element_type=jnp.float32)
            up_act = jnp.dot(normed, up_mat, preferred_element_type=jnp.float32)
            hidden_act = (jax.nn.silu(gate_act) * up_act).astype(jnp.bfloat16)
            partial_value = jnp.dot(hidden_act, down_mat, preferred_element_type=jnp.float32).astype(jnp.bfloat16)
            summed = summed + lax.optimization_barrier(partial_value).astype(jnp.float32)
        expert_out = lax.optimization_barrier(summed.astype(jnp.bfloat16)).astype(jnp.float32)
        weight = lax.optimization_barrier(jnp.sum(jnp.where(expert_ids == expert, gate_share, jnp.zeros_like(gate_share)), axis=1))
        return running + weight[:, None] * expert_out
    running = lax.fori_loop(0, E_FLIGHT, one_expert, jnp.zeros(hidden.shape, jnp.float32))
    return running.astype(jnp.bfloat16)
```

```python
import functools

import jax
import jax.numpy as jnp
from jax import lax
from jax.experimental import pallas as pl
from jax.experimental.pallas import tpu as pltpu
from jax.sharding import PartitionSpec as P

SPLIT = 4
CAP = 16
SLOTS = 2 * SPLIT
CHUNKS = 4
F32 = jnp.float32
BF16 = jnp.bfloat16
MESH = pl.DeviceIdType.MESH


def exclusive(e, j, flight):
    total, bit = 0, 1
    while bit < flight:
        total = total + bit * ((e // bit + j // bit) % 2)
        bit *= 2
    return total


def sent_in(q, k):
    last = SPLIT - 1
    rows = k < 2 * (q + 1)
    r = k - 2 * (q + 1)
    n = last - q
    block = jnp.where(
        rows, jnp.where(k <= q, q - k, k - q - 1), jnp.where(r < n, q + 1 + r, last - (r - n))
    )
    half = jnp.where(rows, jnp.where(k <= q, 0, 1), jnp.where(r < n, 0, 1))
    return rows, block, half


def kernel(
    flight,
    gain_ref,
    ids_ref,
    hidden_hbm,
    router_hbm,
    gate_hbm,
    up_hbm,
    down_hbm,
    moe_ref,
    hidden_v,
    router_v,
    normed_v,
    out_v,
    hilo_v,
    gu_v,
    down_v,
    act_v,
    x_v,
    p_v,
    r_v,
    f_v,
    res_v,
    local_sem,
    p1_send,
    p1_recv,
    move_send,
    move_recv,
    ret_send,
    ret_recv,
):
    dev = lax.axis_index("expert")
    m = dev // flight
    e = dev % flight
    last = SPLIT - 1
    rows, width = hidden_v.shape
    experts = router_v.shape[1]
    slice_width = down_v.shape[0]
    cols = flight * CAP
    half = cols // 2
    part = half // 2
    place_q = (m, last - m)
    beyond = (dev + flight, dev - flight)

    get_hidden = pltpu.make_async_copy(hidden_hbm, hidden_v, local_sem.at[0])
    get_router = pltpu.make_async_copy(router_hbm, router_v, local_sem.at[1])
    weights = [
        pltpu.make_async_copy(gate_hbm.at[0], gu_v.at[:, pl.ds(0, slice_width)], local_sem.at[2]),
        pltpu.make_async_copy(
            up_hbm.at[0], gu_v.at[:, pl.ds(slice_width, slice_width)], local_sem.at[3]
        ),
        pltpu.make_async_copy(down_hbm.at[0], down_v, local_sem.at[4]),
    ]
    get_hidden.start()

    barrier = pltpu.get_barrier_semaphore()

    def greet(target):
        pl.semaphore_signal(barrier, inc=1, device_id={"expert": target}, device_id_type=MESH)

    @pl.loop(1, flight)
    def _(j):
        greet(m * flight + exclusive(e, j, flight))

    @pl.when(m > 0)
    def _():
        greet(dev - flight)

    @pl.when(m < last)
    def _():
        greet(dev + flight)

    def remote(src, dst, ssem, rsem, target):
        return pltpu.make_async_remote_copy(
            src_ref=src,
            dst_ref=dst,
            send_sem=ssem,
            recv_sem=rsem,
            device_id={"expert": target},
            device_id_type=MESH,
        )

    def band(j):
        return pl.ds(pl.multiple_of(j * CAP, CAP), CAP)

    def side(h):
        return pl.ds(pl.multiple_of(h * half, half), half)

    wide = width // 2

    def wide_cols(ch):
        return pl.ds(pl.multiple_of(ch * wide, wide), wide)

    narrow = width // CHUNKS

    def narrow_cols(c):
        return pl.ds(pl.multiple_of(c * narrow, narrow), narrow)

    ids = ids_ref[...]
    earlier = lax.broadcasted_iota(jnp.int32, (rows, rows), 0) < lax.broadcasted_iota(
        jnp.int32, (rows, rows), 1
    )
    earlier = jnp.where(earlier, 1.0, 0.0).astype(BF16)
    named = lax.broadcasted_iota(jnp.int32, (max(8, flight), rows), 0)
    named = exclusive(e, named, max(8, flight)) if flight >= 8 else exclusive(e, named, 8)
    hits = jnp.zeros((max(8, flight), rows), F32)
    for k in range(ids.shape[0]):
        hits = jnp.where(ids[k : k + 1, :] == named, 1.0, hits)
    slot = jnp.dot(hits.astype(BF16), earlier, preferred_element_type=F32)
    row_place = lax.broadcasted_iota(jnp.int32, (CAP, rows), 0).astype(F32)
    dispatch = jnp.concatenate(
        [
            jnp.where((hits[j : j + 1, :] > 0.5) & (slot[j : j + 1, :] == row_place), 1.0, 0.0)
            for j in range(flight)
        ],
        axis=0,
    ).astype(BF16)

    get_hidden.wait()
    get_router.start()
    for copy in weights:
        copy.start()

    gain = gain_ref[...].astype(F32)[None, :]

    @pl.loop(0, rows // CAP)
    def _(i):
        widened = hidden_v[band(i), :].astype(F32)
        inv_rms = lax.rsqrt(jnp.mean(widened * widened, axis=-1, keepdims=True) + 1e-06)
        normed_v[band(i), :] = (widened * inv_rms * gain).astype(BF16)

    pl.semaphore_wait(
        barrier, flight - 1 + jnp.where(m > 0, 1, 0) + jnp.where(m < last, 1, 0)
    )

    def first(j, ch):
        return remote(
            out_v.at[band(j), wide_cols(ch)],
            x_v.at[m, band(j), wide_cols(ch)],
            p1_send.at[j, ch],
            p1_recv.at[j, ch],
            m * flight + exclusive(e, j, flight),
        )

    @pl.loop(0, 2)
    def _(ch):
        picked_rows = jnp.dot(
            dispatch, normed_v[:, wide_cols(ch)], preferred_element_type=F32
        ).astype(BF16)
        out_v[:, wide_cols(ch)] = picked_rows
        x_v[m, pl.ds(0, CAP), wide_cols(ch)] = picked_rows[:CAP, :]

        @pl.loop(1, flight)
        def _(j):
            first(j, ch).start()

    def rows_move(d, k, c, s, h):
        at = pl.ds(pl.multiple_of(h * half + (c // 2) * part, part), part)
        here = x_v.at[s, at, wide_cols(c % 2)]
        return remote(here, here, move_send.at[d, k, c], move_recv.at[d, k, c], beyond[d])

    def sums_move(d, k, c, s, h):
        return remote(
            p_v.at[s, side(h), narrow_cols(c)],
            r_v.at[d, s, side(h), narrow_cols(c)],
            move_send.at[d, k, c],
            move_recv.at[d, k, c],
            beyond[d],
        )

    def gathered(h, c):
        begin = h * (flight // 2) + (c // 2) * (flight // 4)

        @pl.loop(begin, begin + flight // 4)
        def _(j):
            @pl.when(j > 0)
            def _():
                first(j, c % 2).wait_recv()

    @pl.loop(0, CHUNKS)
    def _(c):
        gathered(0, c)
        for d in range(2):

            @pl.when(place_q[d] < last)
            def _():
                rows_move(d, 0, c, m, 0).start()

    get_router.wait()
    logits = jnp.dot(normed_v[...], router_v[...], preferred_element_type=F32)
    shifted = jnp.exp(logits - jnp.max(logits, axis=-1, keepdims=True))
    probs = shifted / jnp.sum(shifted, axis=-1, keepdims=True)
    expert = lax.broadcasted_iota(jnp.int32, (experts, rows), 0)
    chosen = jnp.zeros((experts, rows), F32)
    for k in range(ids.shape[0]):
        chosen = jnp.where(ids[k : k + 1, :] == expert, 1.0, chosen)
    picked = probs * chosen.T
    share = picked / jnp.sum(picked, axis=-1, keepdims=True)
    of_col = exclusive(e, lax.broadcasted_iota(jnp.int32, (experts, cols), 1) // CAP, flight)
    spread = jnp.where(lax.broadcasted_iota(jnp.int32, (experts, cols), 0) == of_col, 1.0, 0.0)
    spread = spread.astype(BF16)
    share_hi = share.astype(BF16)
    share_lo = (share - share_hi.astype(F32)).astype(BF16)
    hi_of = jnp.dot(share_hi, spread, preferred_element_type=F32)
    lo_of = jnp.dot(share_lo, spread, preferred_element_type=F32)
    same = lax.broadcasted_iota(jnp.int32, (rows, rows), 0) == lax.broadcasted_iota(
        jnp.int32, (rows, rows), 1
    )
    select = lax.dot_general(
        jnp.where(same, 1.0, 0.0).astype(BF16),
        dispatch,
        (((1,), (1,)), ((), ())),
        preferred_element_type=F32,
    )
    hilo_v[0] = jnp.where(select > 0.5, hi_of, 0.0).astype(BF16)
    hilo_v[1] = jnp.where(select > 0.5, lo_of, 0.0).astype(BF16)

    def back(j, c):
        return remote(
            f_v.at[band(j), narrow_cols(c)],
            res_v.at[band(j), narrow_cols(c)],
            ret_send.at[j, c],
            ret_recv.at[j, c],
            m * flight + exclusive(e, j, flight),
        )

    def in_pass(d, k):
        q = place_q[d]
        _, block, h = sent_in(q - 1, k - 1)
        s = block if d == 0 else last - block
        arrived = k <= 2 * q
        own_h = jnp.where(k == 2 * q + 1, 0, 1)
        return jnp.where(arrived, s, m), jnp.where(arrived, h, own_h)

    farther = jnp.where(place_q[0] > place_q[1], place_q[0], place_q[1])

    @pl.loop(0, SLOTS)
    def _(k):
        @pl.when(k == 1)
        def _():
            for copy in weights:
                copy.wait()

        @pl.when((k > 0) & (k <= 2 * farther))
        def _():
            s0, h0 = in_pass(0, k)
            s1, h1 = in_pass(1, k)
            both = jnp.concatenate([x_v[s0, side(h0), :], x_v[s1, side(h1), :]], axis=0)
            gu = jnp.dot(both, gu_v[...], preferred_element_type=F32)
            act_v[...] = (jax.nn.silu(gu[:, :slice_width]) * gu[:, slice_width:]).astype(BF16)

            @pl.loop(0, CHUNKS)
            def _(i):
                at = narrow_cols(i)
                product = jnp.dot(
                    act_v[...], down_v[:, at], preferred_element_type=F32
                ).astype(BF16)
                p_v[s0, side(h0), at] = product[:half, :]
                p_v[s1, side(h1), at] = product[half:, :]

        @pl.loop(0, CHUNKS)
        def _(c):
            @pl.when(k == 0)
            def _():
                gathered(1, c)

            for d in range(2):
                q = place_q[d]
                is_rows, block, h = sent_in(q - 1, k)
                s = block if d == 0 else last - block

                @pl.when((q > 0) & is_rows)
                def _():
                    rows_move(d, k, c, s, h).wait_recv()

                    @pl.when(q < last)
                    def _():
                        rows_move(d, k + 1, c, s, h).start()

                @pl.when((q > 0) & jnp.logical_not(is_rows))
                def _():
                    sums_move(d, k, c, s, h).wait_recv()

                    @pl.when(block > q)
                    def _():
                        at = narrow_cols(c)
                        p_v[s, side(h), at] = (
                            p_v[s, side(h), at].astype(F32) + r_v[d, s, side(h), at].astype(F32)
                        ).astype(BF16)
                        sums_move(d, k + 1, c, s, h).start()

                @pl.when((k == 2 * q) & (q < last))
                def _():
                    rows_move(d, k + 1, c, m, 1).start()

                @pl.when((q == 0) & (k > 0) & (k < SLOTS - 1))
                def _():
                    _, begun, bh = sent_in(0, k + 1)
                    sums_move(d, k + 1, c, begun if d == 0 else last - begun, bh).start()

            @pl.when((k == 2 * farther) | (k == SLOTS - 1))
            def _():
                h = jnp.where(k == SLOTS - 1, 1, 0)
                at = narrow_cols(c)
                total = p_v[m, side(h), at].astype(F32)
                above = r_v[jnp.where(m < last, 1, 0), m, side(h), at].astype(F32)
                below = r_v[jnp.where(m > 0, 0, 1), m, side(h), at].astype(F32)
                both = jnp.where((m > 0) & (m < last), 1.0, 0.0)
                total = (total + above + both * below).astype(BF16)
                f_v[side(h), at] = total

                @pl.when(h == 0)
                def _():
                    res_v[pl.ds(0, CAP), at] = total[:CAP, :]

                @pl.loop(h * (flight // 2), (h + 1) * (flight // 2))
                def _(j):
                    @pl.when(j > 0)
                    def _():
                        back(j, c).start()

    @pl.loop(0, CHUNKS)
    def _(c):
        @pl.loop(1, flight)
        def _(j):
            back(j, c).wait_recv()

        at = narrow_cols(c)
        results = res_v[:, at]
        moe_ref[:, at] = (
            jnp.dot(hilo_v[0], results, preferred_element_type=F32)
            + jnp.dot(hilo_v[1], results, preferred_element_type=F32)
        ).astype(BF16)

    @pl.loop(1, flight)
    def _(j):
        for ch in range(2):
            first(j, ch).wait_send()

        @pl.loop(0, CHUNKS)
        def _(c):
            back(j, c).wait_send()

    for d in range(2):

        @pl.when(place_q[d] < last)
        def _():
            @pl.loop(0, SLOTS)
            def _(k):
                @pl.loop(0, CHUNKS)
                def _(c):
                    is_rows, block, h = sent_in(place_q[d], k)
                    s = block if d == 0 else last - block

                    @pl.when(is_rows)
                    def _():
                        rows_move(d, k, c, s, h).wait_send()

                    @pl.when(jnp.logical_not(is_rows))
                    def _():
                        sums_move(d, k, c, s, h).wait_send()


def shards(flight, hidden, norm_gain, router_weight, expert_ids, gate_weight, up_weight, down_weight):
    rows, width = hidden.shape
    experts = router_weight.shape[1]
    cols = flight * CAP
    slice_width = gate_weight.shape[2]
    vmem = pl.BlockSpec(memory_space=pltpu.VMEM)
    hbm = pl.BlockSpec(memory_space=pltpu.HBM)
    dma = pltpu.SemaphoreType.DMA
    return pl.pallas_call(
        functools.partial(kernel, flight),
        out_shape=jax.ShapeDtypeStruct((rows, width), BF16),
        in_specs=[vmem] * 2 + [hbm] * 5,
        out_specs=vmem,
        scratch_shapes=[
            pltpu.VMEM((rows, width), BF16),
            pltpu.VMEM((width, experts), BF16),
            pltpu.VMEM((rows, width), BF16),
            pltpu.VMEM((cols, width), BF16),
            pltpu.VMEM((2, rows, cols), BF16),
            pltpu.VMEM((width, 2 * slice_width), BF16),
            pltpu.VMEM((slice_width, width), BF16),
            pltpu.VMEM((cols, slice_width), BF16),
            pltpu.VMEM((SPLIT, cols, width), BF16),
            pltpu.VMEM((SPLIT, cols, width), BF16),
            pltpu.VMEM((2, SPLIT, cols, width), BF16),
            pltpu.VMEM((cols, width), BF16),
            pltpu.VMEM((cols, width), BF16),
            dma((5,)),
            dma((flight, 2)),
            dma((flight, 2)),
            dma((2, SLOTS, CHUNKS)),
            dma((2, SLOTS, CHUNKS)),
            dma((flight, CHUNKS)),
            dma((flight, CHUNKS)),
        ],
        compiler_params=pltpu.CompilerParams(
            collective_id=0, has_side_effects=True, vmem_limit_bytes=60 * 2**20
        ),
    )(norm_gain, expert_ids.T, hidden, router_weight, gate_weight, up_weight, down_weight)


def solution(mesh):
    flight = mesh.shape["expert"] // SPLIT
    in_specs = (
        P(("group", "expert"), None),
        P(),
        P(),
        P(("group", "expert"), None),
        P("expert", None, None),
        P("expert", None, None),
        P("expert", None, None),
    )
    out_specs = P(("group", "expert"), None)
    return jax.shard_map(
        functools.partial(shards, flight),
        mesh=mesh,
        in_specs=in_specs,
        out_specs=out_specs,
        check_vma=False,
    )
```

```python
import functools

import jax
import jax.numpy as jnp
from jax import lax
from jax.experimental import pallas as pl
from jax.experimental.pallas import tpu as pltpu
from jax.sharding import PartitionSpec as P

SPLIT = 4
CAP = 16
SLOTS = 2 * SPLIT
PARTS = 4
CHUNKS = 4
LAG = 3
F32 = jnp.float32
BF16 = jnp.bfloat16
MESH = pl.DeviceIdType.MESH


def exclusive(e, j, flight):
    total, bit = 0, 1
    while bit < flight:
        total = total + bit * ((e // bit + j // bit) % 2)
        bit *= 2
    return total


def sent_in(q, k):
    last = SPLIT - 1
    rows = k < 2 * (q + 1)
    r = k - 2 * (q + 1)
    n = last - q
    block = jnp.where(
        rows, jnp.where(k <= q, q - k, k - q - 1), jnp.where(r < n, q + 1 + r, last - (r - n))
    )
    half = jnp.where(rows, jnp.where(k <= q, 0, 1), jnp.where(r < n, 0, 1))
    return rows, block, half


def kernel(
    flight,
    gain_ref,
    ids_ref,
    hidden_hbm,
    router_hbm,
    gate_hbm,
    up_hbm,
    down_hbm,
    moe_ref,
    hidden_v,
    router_v,
    normed_v,
    out_v,
    hilo_v,
    gu_v,
    down_v,
    act_v,
    x_v,
    p_v,
    r_v,
    f_v,
    res_v,
    inv_v,
    local_sem,
    p1_send,
    p1_recv,
    move_send,
    move_recv,
    ret_send,
    ret_recv,
):
    dev = lax.axis_index("expert")
    m = dev // flight
    e = dev % flight
    last = SPLIT - 1
    rows, width = hidden_v.shape
    experts = router_v.shape[1]
    slice_width = down_v.shape[0]
    cols = flight * CAP
    half = cols // 2
    part = half // 2
    place_q = (m, last - m)
    beyond = (dev + flight, dev - flight)

    get_hidden = pltpu.make_async_copy(hidden_hbm, hidden_v, local_sem.at[0])
    get_router = pltpu.make_async_copy(router_hbm, router_v, local_sem.at[1])
    weights = [
        pltpu.make_async_copy(gate_hbm.at[0], gu_v.at[:, pl.ds(0, slice_width)], local_sem.at[2]),
        pltpu.make_async_copy(
            up_hbm.at[0], gu_v.at[:, pl.ds(slice_width, slice_width)], local_sem.at[3]
        ),
        pltpu.make_async_copy(down_hbm.at[0], down_v, local_sem.at[4]),
    ]
    get_hidden.start()

    barrier = pltpu.get_barrier_semaphore()

    def greet(target):
        pl.semaphore_signal(barrier, inc=1, device_id={"expert": target}, device_id_type=MESH)

    @pl.loop(1, flight)
    def _(j):
        greet(m * flight + exclusive(e, j, flight))

    @pl.when(m > 0)
    def _():
        greet(dev - flight)

    @pl.when(m < last)
    def _():
        greet(dev + flight)

    def remote(src, dst, ssem, rsem, target):
        return pltpu.make_async_remote_copy(
            src_ref=src,
            dst_ref=dst,
            send_sem=ssem,
            recv_sem=rsem,
            device_id={"expert": target},
            device_id_type=MESH,
        )

    def band(j):
        return pl.ds(pl.multiple_of(j * CAP, CAP), CAP)

    def side(h):
        return pl.ds(pl.multiple_of(h * half, half), half)

    wide = width // 2

    def wide_cols(ch):
        return pl.ds(pl.multiple_of(ch * wide, wide), wide)

    narrow = width // CHUNKS

    def narrow_cols(c):
        return pl.ds(pl.multiple_of(c * narrow, narrow), narrow)

    ids = ids_ref[...]
    earlier = lax.broadcasted_iota(jnp.int32, (rows, rows), 0) < lax.broadcasted_iota(
        jnp.int32, (rows, rows), 1
    )
    earlier = jnp.where(earlier, 1.0, 0.0).astype(BF16)
    named = lax.broadcasted_iota(jnp.int32, (max(8, flight), rows), 0)
    named = exclusive(e, named, max(8, flight)) if flight >= 8 else exclusive(e, named, 8)
    hits = jnp.zeros((max(8, flight), rows), F32)
    for k in range(ids.shape[0]):
        hits = jnp.where(ids[k : k + 1, :] == named, 1.0, hits)
    slot = jnp.dot(hits.astype(BF16), earlier, preferred_element_type=F32)
    row_place = lax.broadcasted_iota(jnp.int32, (CAP, rows), 0).astype(F32)
    dispatch = jnp.concatenate(
        [
            jnp.where((hits[j : j + 1, :] > 0.5) & (slot[j : j + 1, :] == row_place), 1.0, 0.0)
            for j in range(flight)
        ],
        axis=0,
    ).astype(BF16)

    get_hidden.wait()
    get_router.start()
    for copy in weights:
        copy.start()

    gain = gain_ref[...].astype(F32)[None, :]

    squares = jnp.zeros((cols, 1), F32)
    for ch in range(PARTS):
        at = pl.ds(ch * (width // PARTS), width // PARTS)
        picked_rows = jnp.dot(dispatch, hidden_v[:, at], preferred_element_type=F32)
        squares = squares + jnp.sum(picked_rows * picked_rows, axis=-1, keepdims=True)
        out_v[:, at] = picked_rows.astype(BF16)
    inv_v[...] = jnp.broadcast_to(lax.rsqrt(squares / width + 1e-06), inv_v.shape)

    def normalised(j):
        return (out_v[band(j), :].astype(F32) * inv_v[band(j), :1] * gain).astype(BF16)

    x_v[m, pl.ds(0, CAP), :] = normalised(0)

    pl.semaphore_wait(
        barrier, flight - 1 + jnp.where(m > 0, 1, 0) + jnp.where(m < last, 1, 0)
    )

    def first(j, ch):
        return remote(
            out_v.at[band(j), wide_cols(ch)],
            x_v.at[m, band(j), wide_cols(ch)],
            p1_send.at[0],
            p1_recv.at[j, ch],
            m * flight + exclusive(e, j, flight),
        )

    def rows_move(d, k, c, s, h):
        at = pl.ds(pl.multiple_of(h * half + (c // 2) * part, part), part)
        here = x_v.at[s, at, wide_cols(c % 2)]
        return remote(here, here, move_send.at[d], move_recv.at[d, k, c], beyond[d])

    def sums_move(d, k, c, s, h):
        return remote(
            p_v.at[s, side(h), narrow_cols(c)],
            r_v.at[d, s, side(h), narrow_cols(c)],
            move_send.at[d],
            move_recv.at[d, k, c],
            beyond[d],
        )

    def gathered(h, c):
        begin = h * (flight // 2) + (c // 2) * (flight // 4)

        @pl.loop(begin, begin + flight // 4)
        def _(j):
            @pl.when(j > 0)
            def _():
                first(j, c % 2).wait_recv()

    def begin_own(c):
        gathered(0, c)
        for d in range(2):

            @pl.when(place_q[d] < last)
            def _():
                rows_move(d, 0, c, m, 0).start()

    if flight == PARTS:
        begin_own(0)
        begin_own(1)

    @pl.loop(flight // 2, flight + flight // 2 - 1)
    def _(i):
        j = jnp.where(i < flight, i, i - flight + 1)
        out_v[band(j), :] = normalised(j)
        for ch in range(2):
            first(j, ch).start()

    @pl.loop(2 if flight == PARTS else 0, PARTS)
    def _(c):
        begin_own(c)

    @pl.loop(0, rows // CAP)
    def _(i):
        widened = hidden_v[band(i), :].astype(F32)
        inv_rms = lax.rsqrt(jnp.mean(widened * widened, axis=-1, keepdims=True) + 1e-06)
        normed_v[band(i), :] = (widened * inv_rms * gain).astype(BF16)

    get_router.wait()
    logits = jnp.dot(normed_v[...], router_v[...], preferred_element_type=F32)
    shifted = jnp.exp(logits - jnp.max(logits, axis=-1, keepdims=True))
    probs = shifted / jnp.sum(shifted, axis=-1, keepdims=True)
    expert = lax.broadcasted_iota(jnp.int32, (experts, rows), 0)
    chosen = jnp.zeros((experts, rows), F32)
    for k in range(ids.shape[0]):
        chosen = jnp.where(ids[k : k + 1, :] == expert, 1.0, chosen)
    picked = probs * chosen.T
    share = picked / jnp.sum(picked, axis=-1, keepdims=True)
    of_col = exclusive(e, lax.broadcasted_iota(jnp.int32, (experts, cols), 1) // CAP, flight)
    spread = jnp.where(lax.broadcasted_iota(jnp.int32, (experts, cols), 0) == of_col, 1.0, 0.0)
    spread = spread.astype(BF16)
    share_hi = share.astype(BF16)
    share_lo = (share - share_hi.astype(F32)).astype(BF16)
    hi_of = jnp.dot(share_hi, spread, preferred_element_type=F32)
    lo_of = jnp.dot(share_lo, spread, preferred_element_type=F32)
    same = lax.broadcasted_iota(jnp.int32, (rows, rows), 0) == lax.broadcasted_iota(
        jnp.int32, (rows, rows), 1
    )
    select = lax.dot_general(
        jnp.where(same, 1.0, 0.0).astype(BF16),
        dispatch,
        (((1,), (1,)), ((), ())),
        preferred_element_type=F32,
    )
    hilo_v[...] = jnp.concatenate(
        [jnp.where(select > 0.5, hi_of, 0.0), jnp.where(select > 0.5, lo_of, 0.0)], axis=1
    ).astype(BF16)

    def back(j, c):
        return remote(
            f_v.at[band(j), narrow_cols(c)],
            res_v.at[band(j), narrow_cols(c)],
            ret_send.at[0],
            ret_recv.at[c],
            m * flight + exclusive(e, j, flight),
        )

    def in_pass(d, k):
        q = place_q[d]
        _, block, h = sent_in(q - 1, k - 1)
        s = block if d == 0 else last - block
        arrived = k <= 2 * q
        own_h = jnp.where(k == 2 * q + 1, 0, 1)
        return jnp.where(arrived, s, m), jnp.where(arrived, h, own_h)

    farther = jnp.where(place_q[0] > place_q[1], place_q[0], place_q[1])

    def combine(c):
        at = narrow_cols(c)
        others = pl.ds(CAP, cols - CAP)
        remote(
            res_v.at[others, at], res_v.at[others, at], ret_send.at[0], ret_recv.at[c], dev
        ).wait_recv()
        results = res_v[:, at]
        moe_ref[:, at] = jnp.dot(
            hilo_v[...], jnp.concatenate([results, results], axis=0), preferred_element_type=F32
        ).astype(BF16)

    def sums(k, c):
        at = narrow_cols(c)
        for d in range(2):
            q = place_q[d]
            is_rows, block, h = sent_in(q - 1, k)
            s = block if d == 0 else last - block

            @pl.when((q > 0) & jnp.logical_not(is_rows))
            def _():
                sums_move(d, k, c, s, h).wait_recv()

                @pl.when(block > q)
                def _():
                    p_v[s, side(h), at] = (
                        p_v[s, side(h), at].astype(F32) + r_v[d, s, side(h), at].astype(F32)
                    ).astype(BF16)
                    sums_move(d, k + 1, c, s, h).start()

            @pl.when((q == 0) & (k > 0) & (k < SLOTS - 1))
            def _():
                _, begun, bh = sent_in(0, k + 1)
                sums_move(d, k + 1, c, begun if d == 0 else last - begun, bh).start()

        @pl.when((k == 2 * farther) | (k == SLOTS - 1))
        def _():
            h = jnp.where(k == SLOTS - 1, 1, 0)
            total = p_v[m, side(h), at].astype(F32)
            above = r_v[jnp.where(m < last, 1, 0), m, side(h), at].astype(F32)
            below = r_v[jnp.where(m > 0, 0, 1), m, side(h), at].astype(F32)
            both = jnp.where((m > 0) & (m < last), 1.0, 0.0)
            total = (total + above + both * below).astype(BF16)
            f_v[side(h), at] = total

            @pl.when(h == 0)
            def _():
                res_v[pl.ds(0, CAP), at] = total[:CAP, :]

            @pl.loop(h * (flight // 2), (h + 1) * (flight // 2))
            def _(j):
                @pl.when(j > 0)
                def _():
                    back(j, c).start()

        @pl.when((k == SLOTS - 1) & (c >= LAG))
        def _():
            combine(c - LAG)

    @pl.loop(0, SLOTS)
    def _(k):
        @pl.when(k == 1)
        def _():
            for copy in weights:
                copy.wait()

        @pl.when((k > 0) & (k <= 2 * farther))
        def _():
            s0, h0 = in_pass(0, k)
            s1, h1 = in_pass(1, k)
            both = jnp.concatenate([x_v[s0, side(h0), :], x_v[s1, side(h1), :]], axis=0)
            gu = jnp.dot(both, gu_v[...], preferred_element_type=F32)
            act_v[...] = (jax.nn.silu(gu[:, :slice_width]) * gu[:, slice_width:]).astype(BF16)

            @pl.loop(0, PARTS)
            def _(i):
                at = pl.ds(pl.multiple_of(i * (width // PARTS), width // PARTS), width // PARTS)
                product = jnp.dot(
                    act_v[...], down_v[:, at], preferred_element_type=F32
                ).astype(BF16)
                p_v[s0, side(h0), at] = product[:half, :]
                p_v[s1, side(h1), at] = product[half:, :]

        @pl.loop(0, PARTS)
        def _(part_c):
            @pl.when(k == 0)
            def _():
                gathered(1, part_c)

            for d in range(2):
                q = place_q[d]
                is_rows, block, h = sent_in(q - 1, k)
                s = block if d == 0 else last - block

                @pl.when((q > 0) & is_rows)
                def _():
                    rows_move(d, k, part_c, s, h).wait_recv()

                    @pl.when(q < last)
                    def _():
                        rows_move(d, k + 1, part_c, s, h).start()

                @pl.when((k == 2 * q) & (q < last))
                def _():
                    rows_move(d, k + 1, part_c, m, 1).start()

            @pl.loop(part_c * (CHUNKS // PARTS), (part_c + 1) * (CHUNKS // PARTS))
            def _(c):
                sums(k, c)

    @pl.loop(CHUNKS - LAG, CHUNKS)
    def _(c):
        combine(c)

    others = pl.ds(CAP, cols - CAP)
    remote(out_v.at[others], out_v.at[others], p1_send.at[0], p1_recv.at[0, 0], dev).wait_send()
    remote(f_v.at[others], f_v.at[others], ret_send.at[0], ret_recv.at[0], dev).wait_send()
    for d in range(2):

        @pl.when(place_q[d] < last)
        def _():
            remote(x_v, x_v, move_send.at[d], move_recv.at[d, 0, 0], dev).wait_send()


def shards(flight, hidden, norm_gain, router_weight, expert_ids, gate_weight, up_weight, down_weight):
    rows, width = hidden.shape
    experts = router_weight.shape[1]
    cols = flight * CAP
    slice_width = gate_weight.shape[2]
    vmem = pl.BlockSpec(memory_space=pltpu.VMEM)
    hbm = pl.BlockSpec(memory_space=pltpu.HBM)
    dma = pltpu.SemaphoreType.DMA
    blocks = 2 * width * (16 * cols + 4 * cols + 3 * rows + experts + 3 * slice_width)
    grant = max(105 * 2**19, blocks + 2**23)
    return pl.pallas_call(
        functools.partial(kernel, flight),
        out_shape=jax.ShapeDtypeStruct((rows, width), BF16),
        in_specs=[vmem] * 2 + [hbm] * 5,
        out_specs=vmem,
        scratch_shapes=[
            pltpu.VMEM((rows, width), BF16),
            pltpu.VMEM((width, experts), BF16),
            pltpu.VMEM((rows, width), BF16),
            pltpu.VMEM((cols, width), BF16),
            pltpu.VMEM((rows, 2 * cols), BF16),
            pltpu.VMEM((width, 2 * slice_width), BF16),
            pltpu.VMEM((slice_width, width), BF16),
            pltpu.VMEM((cols, slice_width), BF16),
            pltpu.VMEM((SPLIT, cols, width), BF16),
            pltpu.VMEM((SPLIT, cols, width), BF16),
            pltpu.VMEM((2, SPLIT, cols, width), BF16),
            pltpu.VMEM((cols, width), BF16),
            pltpu.VMEM((cols, width), BF16),
            pltpu.VMEM((cols, 128), F32),
            dma((5,)),
            dma((1,)),
            dma((flight, 2)),
            dma((2,)),
            dma((2, SLOTS, CHUNKS)),
            dma((1,)),
            dma((CHUNKS,)),
        ],
        compiler_params=pltpu.CompilerParams(
            collective_id=0, has_side_effects=True, vmem_limit_bytes=grant
        ),
    )(norm_gain, expert_ids.T, hidden, router_weight, gate_weight, up_weight, down_weight)


def solution(mesh):
    flight = mesh.shape["expert"] // SPLIT
    in_specs = (
        P(("group", "expert"), None),
        P(),
        P(),
        P(("group", "expert"), None),
        P("expert", None, None),
        P("expert", None, None),
        P("expert", None, None),
    )
    out_specs = P(("group", "expert"), None)
    return jax.shard_map(
        functools.partial(shards, flight),
        mesh=mesh,
        in_specs=in_specs,
        out_specs=out_specs,
        check_vma=False,
    )
```

```python
import functools

import jax
import jax.numpy as jnp
from jax import lax
from jax.experimental import pallas as pl
from jax.experimental.pallas import tpu as pltpu
from jax.sharding import PartitionSpec as P

SPLIT = 4
CAP = 16
SLOTS = 2 * SPLIT
PARTS = 4
CHUNKS = 4
F32 = jnp.float32
BF16 = jnp.bfloat16
MESH = pl.DeviceIdType.MESH


def exclusive(e, j, flight):
    total, bit = 0, 1
    while bit < flight:
        total = total + bit * ((e // bit + j // bit) % 2)
        bit *= 2
    return total


def partner(e, p, flight):
    return exclusive(e, p // 2 + (p % 2) * (flight // 2), flight)


def sent_in(q, k):
    last = SPLIT - 1
    rows = k < 2 * (q + 1)
    r = k - 2 * (q + 1)
    n = last - q
    block = jnp.where(
        rows, jnp.where(k <= q, q - k, k - q - 1), jnp.where(r < n, q + 1 + r, last - (r - n))
    )
    half = jnp.where(rows, jnp.where(k <= q, 0, 1), jnp.where(r < n, 0, 1))
    return rows, block, half


def kernel(
    flight,
    gain_ref,
    ids_ref,
    hidden_hbm,
    router_hbm,
    gate_hbm,
    up_hbm,
    down_hbm,
    moe_ref,
    hidden_v,
    router_v,
    normed_v,
    out_v,
    hilo_v,
    gu_v,
    down_v,
    act_v,
    x_v,
    p_v,
    r_v,
    fin_v,
    inv_v,
    local_sem,
    p1_send,
    p1_recv,
    move_send,
    move_recv,
    own_send,
    own_recv,
    fin_recv,
):
    dev = lax.axis_index("expert")
    m = dev // flight
    e = dev % flight
    last = SPLIT - 1
    rows, width = hidden_v.shape
    experts = router_v.shape[1]
    slice_width = down_v.shape[0]
    cols = flight * CAP
    half = cols // 2
    part = half // 2
    place_q = (m, last - m)
    beyond = (dev + flight, dev - flight)

    get_hidden = pltpu.make_async_copy(hidden_hbm, hidden_v, local_sem.at[0])
    get_router = pltpu.make_async_copy(router_hbm, router_v, local_sem.at[1])
    weights = [
        pltpu.make_async_copy(gate_hbm.at[0], gu_v.at[:, pl.ds(0, slice_width)], local_sem.at[2]),
        pltpu.make_async_copy(
            up_hbm.at[0], gu_v.at[:, pl.ds(slice_width, slice_width)], local_sem.at[3]
        ),
        pltpu.make_async_copy(down_hbm.at[0], down_v, local_sem.at[4]),
    ]
    get_hidden.start()

    barrier = pltpu.get_barrier_semaphore()

    def greet(target):
        pl.semaphore_signal(barrier, inc=1, device_id={"expert": target}, device_id_type=MESH)

    @pl.loop(1, flight)
    def _(j):
        greet(m * flight + partner(e, j, flight))

    @pl.loop(0, flight)
    def _(j):
        @pl.when(m > 0)
        def _():
            greet((m - 1) * flight + j)

        @pl.when(m < last)
        def _():
            greet((m + 1) * flight + j)

    def remote(src, dst, ssem, rsem, target):
        return pltpu.make_async_remote_copy(
            src_ref=src,
            dst_ref=dst,
            send_sem=ssem,
            recv_sem=rsem,
            device_id={"expert": target},
            device_id_type=MESH,
        )

    def band(j):
        if isinstance(j, int):
            return pl.ds(j * CAP, CAP)
        return pl.ds(pl.multiple_of(j * CAP, CAP), CAP)

    def side(h):
        if isinstance(h, int):
            return pl.ds(h * half, half)
        return pl.ds(pl.multiple_of(h * half, half), half)

    wide = width // 2

    def wide_cols(ch):
        return pl.ds(pl.multiple_of(ch * wide, wide), wide)

    narrow = width // CHUNKS

    def narrow_cols(c):
        if isinstance(c, int):
            return pl.ds(c * narrow, narrow)
        return pl.ds(pl.multiple_of(c * narrow, narrow), narrow)

    ids = ids_ref[...]
    earlier = lax.broadcasted_iota(jnp.int32, (rows, rows), 0) < lax.broadcasted_iota(
        jnp.int32, (rows, rows), 1
    )
    earlier = jnp.where(earlier, 1.0, 0.0).astype(BF16)
    named = lax.broadcasted_iota(jnp.int32, (max(8, flight), rows), 0)
    named = jnp.where(named < flight, partner(e, named % flight, flight), -1)
    hits = jnp.zeros((max(8, flight), rows), F32)
    for k in range(ids.shape[0]):
        hits = jnp.where(ids[k : k + 1, :] == named, 1.0, hits)
    slot = jnp.dot(hits.astype(BF16), earlier, preferred_element_type=F32)
    row_place = lax.broadcasted_iota(jnp.int32, (CAP, rows), 0).astype(F32)
    dispatch = jnp.concatenate(
        [
            jnp.where((hits[j : j + 1, :] > 0.5) & (slot[j : j + 1, :] == row_place), 1.0, 0.0)
            for j in range(flight)
        ],
        axis=0,
    ).astype(BF16)

    get_hidden.wait()
    get_router.start()
    for copy in weights:
        copy.start()

    gain = gain_ref[...].astype(F32)[None, :]

    squares = jnp.zeros((cols, 1), F32)
    for ch in range(PARTS):
        at = pl.ds(ch * (width // PARTS), width // PARTS)
        picked_rows = jnp.dot(dispatch, hidden_v[:, at], preferred_element_type=F32)
        squares = squares + jnp.sum(picked_rows * picked_rows, axis=-1, keepdims=True)
        out_v[:, at] = picked_rows.astype(BF16)
    inv_v[...] = jnp.broadcast_to(lax.rsqrt(squares / width + 1e-06), inv_v.shape)

    def normalised(j):
        return (out_v[band(j), :].astype(F32) * inv_v[band(j), :1] * gain).astype(BF16)

    x_v[m, pl.ds(0, CAP), :] = normalised(0)

    pl.semaphore_wait(
        barrier, flight - 1 + jnp.where(m > 0, flight, 0) + jnp.where(m < last, flight, 0)
    )

    def first(j, ch):
        return remote(
            out_v.at[band(j), wide_cols(ch)],
            x_v.at[m, band(j), wide_cols(ch)],
            p1_send.at[0],
            p1_recv.at[j, ch],
            m * flight + partner(e, j, flight),
        )

    def rows_move(d, k, c, s, h):
        at = pl.ds(pl.multiple_of(h * half + (c // 2) * part, part), part)
        here = x_v.at[s, at, wide_cols(c % 2)]
        return remote(here, here, move_send.at[d], move_recv.at[d, k, c], beyond[d])

    def sums_move(d, k, c, s, h):
        return remote(
            p_v.at[s, side(h), narrow_cols(c)],
            r_v.at[d, s, side(h), narrow_cols(c)],
            move_send.at[d],
            move_recv.at[d, k, c],
            beyond[d],
        )

    def gathered(h, c):
        begin = h * (flight // 2) + (c // 2) * (flight // 4)

        @pl.loop(begin, begin + flight // 4)
        def _(j):
            @pl.when(j > 0)
            def _():
                first(j, c % 2).wait_recv()

    def begin_own(c):
        gathered(0, c)
        for d in range(2):

            @pl.when(place_q[d] < last)
            def _():
                rows_move(d, 0, c, m, 0).start()

    def begin_band(j):
        out_v[band(j), :] = normalised(j)
        for ch in range(2):
            first(j, ch).start()

    @pl.loop(1, flight // 2)
    def _(j):
        begin_band(j)

    @pl.loop(0, PARTS)
    def _(c):
        begin_own(c)

    @pl.loop(0, flight // 2)
    def _(i):
        begin_band(flight - 1 - i)

    @pl.loop(0, rows // CAP)
    def _(i):
        widened = hidden_v[band(i), :].astype(F32)
        inv_rms = lax.rsqrt(jnp.mean(widened * widened, axis=-1, keepdims=True) + 1e-06)
        normed_v[band(i), :] = (widened * inv_rms * gain).astype(BF16)

    get_router.wait()
    logits = jnp.dot(normed_v[...], router_v[...], preferred_element_type=F32)
    shifted = jnp.exp(logits - jnp.max(logits, axis=-1, keepdims=True))
    probs = shifted / jnp.sum(shifted, axis=-1, keepdims=True)
    expert = lax.broadcasted_iota(jnp.int32, (experts, rows), 0)
    chosen = jnp.zeros((experts, rows), F32)
    for k in range(ids.shape[0]):
        chosen = jnp.where(ids[k : k + 1, :] == expert, 1.0, chosen)
    picked = probs * chosen.T
    share = picked / jnp.sum(picked, axis=-1, keepdims=True)
    of_col = partner(e, lax.broadcasted_iota(jnp.int32, (experts, cols), 1) // CAP, flight)
    spread = jnp.where(lax.broadcasted_iota(jnp.int32, (experts, cols), 0) == of_col, 1.0, 0.0)
    spread = spread.astype(BF16)
    share_hi = share.astype(BF16)
    share_lo = (share - share_hi.astype(F32)).astype(BF16)
    hi_of = jnp.dot(share_hi, spread, preferred_element_type=F32)
    lo_of = jnp.dot(share_lo, spread, preferred_element_type=F32)
    same = lax.broadcasted_iota(jnp.int32, (rows, rows), 0) == lax.broadcasted_iota(
        jnp.int32, (rows, rows), 1
    )
    select = lax.dot_general(
        jnp.where(same, 1.0, 0.0).astype(BF16),
        dispatch,
        (((1,), (1,)), ((), ())),
        preferred_element_type=F32,
    )
    hilo_v[...] = jnp.concatenate(
        [jnp.where(select > 0.5, hi_of, 0.0), jnp.where(select > 0.5, lo_of, 0.0)], axis=1
    ).astype(BF16)

    def own_move(j):
        return remote(
            p_v.at[m, band(j)],
            fin_v.at[2, band(j)],
            own_send.at[0],
            own_recv.at[0],
            m * flight + partner(e, j, flight),
        )

    def final_move(d, c, j, h):
        there = m + 1 if d == 0 else m - 1
        return remote(
            p_v.at[there, band(j), narrow_cols(c)],
            fin_v.at[d, band(j), narrow_cols(c)],
            move_send.at[d],
            fin_recv.at[d, h, c],
            there * flight + partner(e, j, flight),
        )

    def send_sum(d, k, c, s, block, h):
        @pl.when(block == place_q[d] + 1)
        def _():
            @pl.loop(h * (flight // 2), (h + 1) * (flight // 2))
            def _(j):
                final_move(d, c, j, h).start()

        @pl.when(block > place_q[d] + 1)
        def _():
            sums_move(d, k, c, s, h).start()

    def in_pass(d, k):
        q = place_q[d]
        _, block, h = sent_in(q - 1, k - 1)
        s = block if d == 0 else last - block
        return s, h

    farther = jnp.where(place_q[0] > place_q[1], place_q[0], place_q[1])
    nearer = last - farther

    def combine(c):
        at = narrow_cols(c)
        for d in range(2):

            @pl.when(place_q[d] > 0)
            def _():
                for h in range(2):
                    here = fin_v.at[d, side(h), at]
                    remote(here, here, move_send.at[d], fin_recv.at[d, h, c], dev).wait_recv()

        total = fin_v[2, :, at].astype(F32)
        above = fin_v[jnp.where(m < last, 1, 0), :, at].astype(F32)
        below = fin_v[jnp.where(m > 0, 0, 1), :, at].astype(F32)
        both = jnp.where((m > 0) & (m < last), 1.0, 0.0)
        results = (total + above + both * below).astype(BF16)
        moe_ref[:, at] = jnp.dot(
            hilo_v[...], jnp.concatenate([results, results], axis=0), preferred_element_type=F32
        ).astype(BF16)

    def sums(k, c):
        at = narrow_cols(c)
        for d in range(2):
            q = place_q[d]
            is_rows, block, h = sent_in(q - 1, k)
            s = block if d == 0 else last - block

            @pl.when((q > 0) & jnp.logical_not(is_rows) & (block > q))
            def _():
                sums_move(d, k, c, s, h).wait_recv()
                p_v[s, side(h), at] = (
                    p_v[s, side(h), at].astype(F32) + r_v[d, s, side(h), at].astype(F32)
                ).astype(BF16)
                send_sum(d, k + 1, c, s, block, h)

            @pl.when((q == 0) & (k > 0))
            def _():
                _, begun, bh = sent_in(0, k + 1)
                send_sum(d, k + 1, c, begun if d == 0 else last - begun, begun, bh)

    @pl.loop(0, SLOTS - 1)
    def _(k):
        @pl.when(k == 1)
        def _():
            for copy in weights:
                copy.wait()

        @pl.when((k > 0) & (k <= 2 * farther))
        def _():
            s0, h0 = in_pass(0, k)
            s1, h1 = in_pass(1, k)
            up_far = place_q[0] > place_q[1]
            sf, hf = jnp.where(up_far, s0, s1), jnp.where(up_far, h0, h1)
            sn, hn = jnp.where(up_far, s1, s0), jnp.where(up_far, h1, h0)
            own = (k == 2 * nearer + 1) | (k == 2 * nearer + 2)
            s0, h0 = sf, hf
            s1 = jnp.where(k <= 2 * nearer, sn, jnp.where(own, m, sf))
            h1 = jnp.where(k <= 2 * nearer, hn, jnp.where(own, k - 2 * nearer - 1, hf))
            both = jnp.concatenate([x_v[s0, side(h0), :], x_v[s1, side(h1), :]], axis=0)
            gu = jnp.dot(both, gu_v[...], preferred_element_type=F32)
            act_v[...] = (jax.nn.silu(gu[:, :slice_width]) * gu[:, slice_width:]).astype(BF16)

            @pl.loop(0, PARTS)
            def _(i):
                at = pl.ds(pl.multiple_of(i * (width // PARTS), width // PARTS), width // PARTS)
                product = jnp.dot(
                    act_v[...], down_v[:, at], preferred_element_type=F32
                ).astype(BF16)
                p_v[s0, side(h0), at] = product[:half, :]
                p_v[s1, side(h1), at] = product[half:, :]

        for h in range(2):

            @pl.when(k == 2 * nearer + 1 + h)
            def _():
                if h == 0:
                    fin_v[2, band(0), :] = p_v[m, band(0), :]
                for j in range(max(1, h * (flight // 2)), (h + 1) * (flight // 2)):
                    own_move(j).start()

        @pl.loop(0, PARTS)
        def _(part_c):
            @pl.when(k == 0)
            def _():
                gathered(1, part_c)

            for d in range(2):
                q = place_q[d]
                is_rows, block, h = sent_in(q - 1, k)
                s = block if d == 0 else last - block

                @pl.when((q > 0) & is_rows)
                def _():
                    rows_move(d, k, part_c, s, h).wait_recv()

                    @pl.when(q < last)
                    def _():
                        rows_move(d, k + 1, part_c, s, h).start()

                @pl.when((k == 2 * q) & (q < last))
                def _():
                    rows_move(d, k + 1, part_c, m, 1).start()

            @pl.loop(part_c * (CHUNKS // PARTS), (part_c + 1) * (CHUNKS // PARTS))
            def _(c):
                sums(k, c)

    others = pl.ds(CAP, cols - CAP)
    remote(
        fin_v.at[2, others], fin_v.at[2, others], own_send.at[0], own_recv.at[0], dev
    ).wait_recv()
    for c in range(CHUNKS):
        combine(c)

    remote(out_v.at[others], out_v.at[others], p1_send.at[0], p1_recv.at[0, 0], dev).wait_send()
    remote(p_v.at[m, others], p_v.at[m, others], own_send.at[0], own_recv.at[0], dev).wait_send()
    for d in range(2):

        @pl.when(place_q[d] < last)
        def _():
            remote(x_v, x_v, move_send.at[d], move_recv.at[d, 0, 0], dev).wait_send()


def shards(flight, hidden, norm_gain, router_weight, expert_ids, gate_weight, up_weight, down_weight):
    rows, width = hidden.shape
    experts = router_weight.shape[1]
    cols = flight * CAP
    slice_width = gate_weight.shape[2]
    vmem = pl.BlockSpec(memory_space=pltpu.VMEM)
    hbm = pl.BlockSpec(memory_space=pltpu.HBM)
    dma = pltpu.SemaphoreType.DMA
    blocks = 2 * width * (16 * cols + 4 * cols + 3 * rows + experts + 3 * slice_width)
    grant = max(105 * 2**19, blocks + 2**23)
    return pl.pallas_call(
        functools.partial(kernel, flight),
        out_shape=jax.ShapeDtypeStruct((rows, width), BF16),
        in_specs=[vmem] * 2 + [hbm] * 5,
        out_specs=vmem,
        scratch_shapes=[
            pltpu.VMEM((rows, width), BF16),
            pltpu.VMEM((width, experts), BF16),
            pltpu.VMEM((rows, width), BF16),
            pltpu.VMEM((cols, width), BF16),
            pltpu.VMEM((rows, 2 * cols), BF16),
            pltpu.VMEM((width, 2 * slice_width), BF16),
            pltpu.VMEM((slice_width, width), BF16),
            pltpu.VMEM((cols, slice_width), BF16),
            pltpu.VMEM((SPLIT, cols, width), BF16),
            pltpu.VMEM((SPLIT, cols, width), BF16),
            pltpu.VMEM((2, SPLIT, cols, width), BF16),
            pltpu.VMEM((3, cols, width), BF16),
            pltpu.VMEM((cols, 128), F32),
            dma((5,)),
            dma((1,)),
            dma((flight, 2)),
            dma((2,)),
            dma((2, SLOTS, CHUNKS)),
            dma((1,)),
            dma((1,)),
            dma((2, 2, CHUNKS)),
        ],
        compiler_params=pltpu.CompilerParams(
            collective_id=0, has_side_effects=True, vmem_limit_bytes=grant
        ),
    )(norm_gain, expert_ids.T, hidden, router_weight, gate_weight, up_weight, down_weight)


def solution(mesh):
    flight = mesh.shape["expert"] // SPLIT
    in_specs = (
        P(("group", "expert"), None),
        P(),
        P(),
        P(("group", "expert"), None),
        P("expert", None, None),
        P("expert", None, None),
        P("expert", None, None),
    )
    out_specs = P(("group", "expert"), None)
    return jax.shard_map(
        functools.partial(shards, flight),
        mesh=mesh,
        in_specs=in_specs,
        out_specs=out_specs,
        check_vma=False,
    )
```

```python
import functools

import jax
import jax.numpy as jnp
from jax import lax
from jax.experimental import pallas as pl
from jax.experimental.pallas import tpu as pltpu
from jax.sharding import PartitionSpec as P

SPLIT = 4
CAP = 16
SLOTS = 2 * SPLIT
PARTS = 4
CHUNKS = 2
ENDS = 4
F32 = jnp.float32
BF16 = jnp.bfloat16
MESH = pl.DeviceIdType.MESH


def exclusive(e, j, flight):
    total, bit = 0, 1
    while bit < flight:
        total = total + bit * ((e // bit + j // bit) % 2)
        bit *= 2
    return total


def partner(e, p, flight):
    return exclusive(e, p // 2 + (p % 2) * (flight // 2), flight)


def sent_in(q, k):
    last = SPLIT - 1
    rows = k < 2 * (q + 1)
    r = k - 2 * (q + 1)
    n = last - q
    block = jnp.where(
        rows, jnp.where(k <= q, q - k, k - q - 1), jnp.where(r < n, q + 1 + r, last - (r - n))
    )
    half = jnp.where(rows, jnp.where(k <= q, 0, 1), jnp.where(r < n, 0, 1))
    return rows, block, half


def kernel(
    flight,
    gain_ref,
    ids_ref,
    hidden_hbm,
    router_hbm,
    gate_hbm,
    up_hbm,
    down_hbm,
    moe_ref,
    hidden_v,
    router_v,
    normed_v,
    out_v,
    hilo_v,
    gu_v,
    down_v,
    act_v,
    x_v,
    p_v,
    r_v,
    fin_v,
    inv_v,
    local_sem,
    p1_send,
    p1_recv,
    move_send,
    move_recv,
    own_send,
    own_recv,
    fin_recv,
):
    dev = lax.axis_index("expert")
    m = dev // flight
    e = dev % flight
    last = SPLIT - 1
    rows, width = hidden_v.shape
    experts = router_v.shape[1]
    slice_width = down_v.shape[0]
    cols = flight * CAP
    half = cols // 2
    part = half // 2
    place_q = (m, last - m)
    beyond = (dev + flight, dev - flight)

    def get_hidden(i):
        at = pl.ds(i * (width // PARTS), width // PARTS)
        return pltpu.make_async_copy(hidden_hbm.at[:, at], hidden_v.at[:, at], local_sem.at[4 + i])

    get_router = pltpu.make_async_copy(router_hbm, router_v, local_sem.at[0])
    weights = [
        pltpu.make_async_copy(gate_hbm.at[0], gu_v.at[:, pl.ds(0, slice_width)], local_sem.at[1]),
        pltpu.make_async_copy(
            up_hbm.at[0], gu_v.at[:, pl.ds(slice_width, slice_width)], local_sem.at[2]
        ),
        pltpu.make_async_copy(down_hbm.at[0], down_v, local_sem.at[3]),
    ]
    for i in range(PARTS):
        get_hidden(i).start()

    barrier = pltpu.get_barrier_semaphore()

    def greet(target):
        pl.semaphore_signal(barrier, inc=1, device_id={"expert": target}, device_id_type=MESH)

    @pl.loop(1, flight)
    def _(j):
        greet(m * flight + partner(e, j, flight))

    @pl.loop(0, flight)
    def _(j):
        @pl.when(m > 0)
        def _():
            greet((m - 1) * flight + j)

        @pl.when(m < last)
        def _():
            greet((m + 1) * flight + j)

    def remote(src, dst, ssem, rsem, target):
        return pltpu.make_async_remote_copy(
            src_ref=src,
            dst_ref=dst,
            send_sem=ssem,
            recv_sem=rsem,
            device_id={"expert": target},
            device_id_type=MESH,
        )

    def band(j):
        if isinstance(j, int):
            return pl.ds(j * CAP, CAP)
        return pl.ds(pl.multiple_of(j * CAP, CAP), CAP)

    def side(h):
        if isinstance(h, int):
            return pl.ds(h * half, half)
        return pl.ds(pl.multiple_of(h * half, half), half)

    wide = width // 2

    def wide_cols(ch):
        return pl.ds(pl.multiple_of(ch * wide, wide), wide)

    narrow = width // CHUNKS

    final = width // ENDS

    def final_cols(c):
        if isinstance(c, int):
            return pl.ds(c * final, final)
        return pl.ds(pl.multiple_of(c * final, final), final)

    def narrow_cols(c):
        if isinstance(c, int):
            return pl.ds(c * narrow, narrow)
        return pl.ds(pl.multiple_of(c * narrow, narrow), narrow)

    ids = ids_ref[...]
    earlier = lax.broadcasted_iota(jnp.int32, (rows, rows), 0) < lax.broadcasted_iota(
        jnp.int32, (rows, rows), 1
    )
    earlier = jnp.where(earlier, 1.0, 0.0).astype(BF16)
    named = lax.broadcasted_iota(jnp.int32, (max(8, flight), rows), 0)
    named = jnp.where(named < flight, partner(e, named % flight, flight), -1)
    hits = jnp.zeros((max(8, flight), rows), F32)
    for k in range(ids.shape[0]):
        hits = jnp.where(ids[k : k + 1, :] == named, 1.0, hits)
    slot = jnp.dot(hits.astype(BF16), earlier, preferred_element_type=F32)
    row_place = lax.broadcasted_iota(jnp.int32, (CAP, rows), 0).astype(F32)
    dispatch = jnp.concatenate(
        [
            jnp.where((hits[j : j + 1, :] > 0.5) & (slot[j : j + 1, :] == row_place), 1.0, 0.0)
            for j in range(flight)
        ],
        axis=0,
    ).astype(BF16)

    gain = gain_ref[...].astype(F32)[None, :]

    squares = jnp.zeros((cols, 1), F32)
    for ch in range(PARTS):
        at = pl.ds(ch * (width // PARTS), width // PARTS)
        get_hidden(ch).wait()
        picked_rows = jnp.dot(dispatch, hidden_v[:, at], preferred_element_type=F32)
        squares = squares + jnp.sum(picked_rows * picked_rows, axis=-1, keepdims=True)
        out_v[:, at] = picked_rows.astype(BF16)
    get_router.start()
    for copy in weights:
        copy.start()
    inv_v[...] = jnp.broadcast_to(lax.rsqrt(squares / width + 1e-06), inv_v.shape)

    def normalised(j):
        return (out_v[band(j), :].astype(F32) * inv_v[band(j), :1] * gain).astype(BF16)

    x_v[m, pl.ds(0, CAP), :] = normalised(0)

    pl.semaphore_wait(
        barrier, flight - 1 + jnp.where(m > 0, flight, 0) + jnp.where(m < last, flight, 0)
    )

    def first(j, ch):
        return remote(
            out_v.at[band(j), wide_cols(ch)],
            x_v.at[m, band(j), wide_cols(ch)],
            p1_send.at[0],
            p1_recv.at[j, ch],
            m * flight + partner(e, j, flight),
        )

    def rows_move(d, k, c, s, h):
        at = pl.ds(pl.multiple_of(h * half + (c // 2) * part, part), part)
        here = x_v.at[s, at, wide_cols(c % 2)]
        return remote(here, here, move_send.at[d], move_recv.at[d, k, c], beyond[d])

    def sums_move(d, k, c, s, h):
        return remote(
            p_v.at[s, side(h), narrow_cols(c)],
            r_v.at[d, s, side(h), narrow_cols(c)],
            move_send.at[d],
            move_recv.at[d, k, c],
            beyond[d],
        )

    def gathered(h, c):
        begin = h * (flight // 2) + (c // 2) * (flight // 4)

        @pl.loop(begin, begin + flight // 4)
        def _(j):
            @pl.when(j > 0)
            def _():
                first(j, c % 2).wait_recv()

    def begin_own(c):
        gathered(0, c)
        for d in range(2):

            @pl.when(place_q[d] < last)
            def _():
                rows_move(d, 0, c, m, 0).start()

    def begin_band(j):
        out_v[band(j), :] = normalised(j)
        for ch in range(2):
            first(j, ch).start()

    @pl.loop(1, flight // 2)
    def _(j):
        begin_band(j)

    @pl.loop(0, PARTS)
    def _(c):
        begin_own(c)

    @pl.loop(0, flight // 2)
    def _(i):
        begin_band(flight - 1 - i)

    @pl.loop(0, rows // CAP)
    def _(i):
        widened = hidden_v[band(i), :].astype(F32)
        inv_rms = lax.rsqrt(jnp.mean(widened * widened, axis=-1, keepdims=True) + 1e-06)
        normed_v[band(i), :] = (widened * inv_rms * gain).astype(BF16)

    get_router.wait()
    logits = jnp.dot(normed_v[...], router_v[...], preferred_element_type=F32)
    shifted = jnp.exp(logits - jnp.max(logits, axis=-1, keepdims=True))
    probs = shifted / jnp.sum(shifted, axis=-1, keepdims=True)
    expert = lax.broadcasted_iota(jnp.int32, (experts, rows), 0)
    chosen = jnp.zeros((experts, rows), F32)
    for k in range(ids.shape[0]):
        chosen = jnp.where(ids[k : k + 1, :] == expert, 1.0, chosen)
    picked = probs * chosen.T
    share = picked / jnp.sum(picked, axis=-1, keepdims=True)
    of_col = partner(e, lax.broadcasted_iota(jnp.int32, (experts, cols), 1) // CAP, flight)
    spread = jnp.where(lax.broadcasted_iota(jnp.int32, (experts, cols), 0) == of_col, 1.0, 0.0)
    spread = spread.astype(BF16)
    share_hi = share.astype(BF16)
    share_lo = (share - share_hi.astype(F32)).astype(BF16)
    hi_of = jnp.dot(share_hi, spread, preferred_element_type=F32)
    lo_of = jnp.dot(share_lo, spread, preferred_element_type=F32)
    same = lax.broadcasted_iota(jnp.int32, (rows, rows), 0) == lax.broadcasted_iota(
        jnp.int32, (rows, rows), 1
    )
    select = lax.dot_general(
        jnp.where(same, 1.0, 0.0).astype(BF16),
        dispatch,
        (((1,), (1,)), ((), ())),
        preferred_element_type=F32,
    )
    hilo_v[...] = jnp.concatenate(
        [jnp.where(select > 0.5, hi_of, 0.0), jnp.where(select > 0.5, lo_of, 0.0)], axis=1
    ).astype(BF16)

    def own_move(j):
        return remote(
            p_v.at[m, band(j)],
            fin_v.at[2, band(j)],
            own_send.at[0],
            own_recv.at[0],
            m * flight + partner(e, j, flight),
        )

    def final_move(d, c, j, h):
        there = m + 1 if d == 0 else m - 1
        return remote(
            p_v.at[there, band(j), final_cols(c)],
            fin_v.at[d, band(j), final_cols(c)],
            move_send.at[d],
            fin_recv.at[d, h, c],
            there * flight + partner(e, j, flight),
        )

    def send_sum(d, k, c, s, block, h):
        @pl.when(block == place_q[d] + 1)
        def _():
            @pl.loop(0, flight // 2)
            def _(i):
                even = flight // 4
                j = h * (flight // 2) + jnp.where(i < even, 2 * i + 1, 2 * (i - even))

                @pl.loop(c * (ENDS // CHUNKS), (c + 1) * (ENDS // CHUNKS))
                def _(end_c):
                    final_move(d, end_c, j, h).start()

        @pl.when(block > place_q[d] + 1)
        def _():
            sums_move(d, k, c, s, h).start()

    def in_pass(d, k):
        q = place_q[d]
        _, block, h = sent_in(q - 1, k - 1)
        s = block if d == 0 else last - block
        return s, h

    farther = jnp.where(place_q[0] > place_q[1], place_q[0], place_q[1])
    nearer = last - farther

    def combine(c):
        at = final_cols(c)
        for d in range(2):

            @pl.when(place_q[d] > 0)
            def _():
                for h in range(2):
                    here = fin_v.at[d, side(h), at]
                    remote(here, here, move_send.at[d], fin_recv.at[d, h, c], dev).wait_recv()

        total = fin_v[2, :, at].astype(F32)
        above = fin_v[jnp.where(m < last, 1, 0), :, at].astype(F32)
        below = fin_v[jnp.where(m > 0, 0, 1), :, at].astype(F32)
        both = jnp.where((m > 0) & (m < last), 1.0, 0.0)
        results = (total + above + both * below).astype(BF16)
        moe_ref[:, at] = jnp.dot(
            hilo_v[...], jnp.concatenate([results, results], axis=0), preferred_element_type=F32
        ).astype(BF16)

    def sums(k, c, coming, begun, bh):
        at = narrow_cols(c)
        for d in range(2):
            q = place_q[d]
            _, is_sum, block, h, s = coming[d]

            @pl.when(is_sum)
            def _():
                sums_move(d, k, c, s, h).wait_recv()
                p_v[s, side(h), at] = (
                    p_v[s, side(h), at].astype(F32) + r_v[d, s, side(h), at].astype(F32)
                ).astype(BF16)
                send_sum(d, k + 1, c, s, block, h)

            @pl.when((q == 0) & (k > 0))
            def _():
                send_sum(d, k + 1, c, begun if d == 0 else last - begun, begun, bh)

    @pl.loop(0, SLOTS - 1)
    def _(k):
        @pl.when(k == 1)
        def _():
            for copy in weights:
                copy.wait()

        @pl.when((k > 0) & (k <= 2 * farther))
        def _():
            s0, h0 = in_pass(0, k)
            s1, h1 = in_pass(1, k)
            up_far = place_q[0] > place_q[1]
            sf, hf = jnp.where(up_far, s0, s1), jnp.where(up_far, h0, h1)
            sn, hn = jnp.where(up_far, s1, s0), jnp.where(up_far, h1, h0)
            own = (k == 2 * nearer + 1) | (k == 2 * nearer + 2)
            s0, h0 = sf, hf
            s1 = jnp.where(k <= 2 * nearer, sn, jnp.where(own, m, sf))
            h1 = jnp.where(k <= 2 * nearer, hn, jnp.where(own, k - 2 * nearer - 1, hf))
            both = jnp.concatenate([x_v[s0, side(h0), :], x_v[s1, side(h1), :]], axis=0)
            gu = jnp.dot(both, gu_v[...], preferred_element_type=F32)
            act_v[...] = (jax.nn.silu(gu[:, :slice_width]) * gu[:, slice_width:]).astype(BF16)

            @pl.loop(0, PARTS)
            def _(i):
                at = pl.ds(pl.multiple_of(i * (width // PARTS), width // PARTS), width // PARTS)
                product = jnp.dot(
                    act_v[...], down_v[:, at], preferred_element_type=F32
                ).astype(BF16)
                p_v[s0, side(h0), at] = product[:half, :]
                p_v[s1, side(h1), at] = product[half:, :]

        for h in range(2):

            @pl.when(k == 2 * nearer + 1 + h)
            def _():
                if h == 0:
                    fin_v[2, band(0), :] = p_v[m, band(0), :]
                for j in range(max(1, h * (flight // 2)), (h + 1) * (flight // 2)):
                    own_move(j).start()

        coming = []
        for d in range(2):
            q = place_q[d]
            rows_in, block, h = sent_in(q - 1, k)
            is_rows = (q > 0) & rows_in
            is_sum = (q > 0) & jnp.logical_not(rows_in) & (block > q)
            coming.append((is_rows, is_sum, block, h, block if d == 0 else last - block))
        _, begun, bh = sent_in(0, k + 1)

        @pl.loop(0, PARTS)
        def _(part_c):
            @pl.when(k == 0)
            def _():
                gathered(1, part_c)

            for d in range(2):
                q = place_q[d]
                is_rows, _, _, h, s = coming[d]

                @pl.when(is_rows)
                def _():
                    rows_move(d, k, part_c, s, h).wait_recv()

                    @pl.when(q < last)
                    def _():
                        rows_move(d, k + 1, part_c, s, h).start()

                @pl.when((k == 2 * q) & (q < last))
                def _():
                    rows_move(d, k + 1, part_c, m, 1).start()

            @pl.when(part_c % (PARTS // CHUNKS) == PARTS // CHUNKS - 1)
            def _():
                c = part_c // (PARTS // CHUNKS)
                sums(k, c, coming, begun, bh)

    others = pl.ds(CAP, cols - CAP)
    remote(
        fin_v.at[2, others], fin_v.at[2, others], own_send.at[0], own_recv.at[0], dev
    ).wait_recv()
    for c in range(ENDS):
        combine(c)

    remote(out_v.at[others], out_v.at[others], p1_send.at[0], p1_recv.at[0, 0], dev).wait_send()
    remote(p_v.at[m, others], p_v.at[m, others], own_send.at[0], own_recv.at[0], dev).wait_send()
    for d in range(2):

        @pl.when(place_q[d] < last)
        def _():
            remote(x_v, x_v, move_send.at[d], move_recv.at[d, 0, 0], dev).wait_send()


def shards(flight, hidden, norm_gain, router_weight, expert_ids, gate_weight, up_weight, down_weight):
    rows, width = hidden.shape
    experts = router_weight.shape[1]
    cols = flight * CAP
    slice_width = gate_weight.shape[2]
    vmem = pl.BlockSpec(memory_space=pltpu.VMEM)
    hbm = pl.BlockSpec(memory_space=pltpu.HBM)
    dma = pltpu.SemaphoreType.DMA
    blocks = 2 * width * (16 * cols + 4 * cols + 3 * rows + experts + 3 * slice_width)
    grant = max(105 * 2**19, blocks + 2**23)
    return pl.pallas_call(
        functools.partial(kernel, flight),
        out_shape=jax.ShapeDtypeStruct((rows, width), BF16),
        in_specs=[vmem] * 2 + [hbm] * 5,
        out_specs=vmem,
        scratch_shapes=[
            pltpu.VMEM((rows, width), BF16),
            pltpu.VMEM((width, experts), BF16),
            pltpu.VMEM((rows, width), BF16),
            pltpu.VMEM((cols, width), BF16),
            pltpu.VMEM((rows, 2 * cols), BF16),
            pltpu.VMEM((width, 2 * slice_width), BF16),
            pltpu.VMEM((slice_width, width), BF16),
            pltpu.VMEM((cols, slice_width), BF16),
            pltpu.VMEM((SPLIT, cols, width), BF16),
            pltpu.VMEM((SPLIT, cols, width), BF16),
            pltpu.VMEM((2, SPLIT, cols, width), BF16),
            pltpu.VMEM((3, cols, width), BF16),
            pltpu.VMEM((cols, 128), F32),
            dma((4 + PARTS,)),
            dma((1,)),
            dma((flight, 2)),
            dma((2,)),
            dma((2, SLOTS, max(PARTS, CHUNKS))),
            dma((1,)),
            dma((1,)),
            dma((2, 2, ENDS)),
        ],
        compiler_params=pltpu.CompilerParams(
            collective_id=0, has_side_effects=True, vmem_limit_bytes=grant
        ),
    )(norm_gain, expert_ids.T, hidden, router_weight, gate_weight, up_weight, down_weight)


def solution(mesh):
    flight = mesh.shape["expert"] // SPLIT
    in_specs = (
        P(("group", "expert"), None),
        P(),
        P(),
        P(("group", "expert"), None),
        P("expert", None, None),
        P("expert", None, None),
        P("expert", None, None),
    )
    out_specs = P(("group", "expert"), None)
    return jax.shard_map(
        functools.partial(shards, flight),
        mesh=mesh,
        in_specs=in_specs,
        out_specs=out_specs,
        check_vma=False,
    )
```

```python
import functools

import jax
import jax.numpy as jnp
from jax import lax
from jax.experimental import pallas as pl
from jax.experimental.pallas import tpu as pltpu
from jax.sharding import PartitionSpec as P

SPLIT = 4
CAP = 16
SLOTS = 2 * SPLIT
PARTS = 4
CHUNKS = 2
ENDS = 4
F32 = jnp.float32
BF16 = jnp.bfloat16
MESH = pl.DeviceIdType.MESH


def exclusive(e, j, flight):
    total, bit = 0, 1
    while bit < flight:
        total = total + bit * ((e // bit + j // bit) % 2)
        bit *= 2
    return total


def partner(e, p, flight):
    return exclusive(e, p // 2 + (p % 2) * (flight // 2), flight)


def sent_in(q, k):
    last = SPLIT - 1
    rows = k < 2 * (q + 1)
    r = k - 2 * (q + 1)
    n = last - q
    block = jnp.where(
        rows, jnp.where(k <= q, q - k, k - q - 1), jnp.where(r < n, q + 1 + r, last - (r - n))
    )
    half = jnp.where(rows, jnp.where(k <= q, 0, 1), jnp.where(r < n, 0, 1))
    return rows, block, half


def kernel(
    flight,
    gain_ref,
    ids_ref,
    hidden_hbm,
    router_hbm,
    gate_hbm,
    up_hbm,
    down_hbm,
    moe_ref,
    hidden_v,
    router_v,
    normed_v,
    out_v,
    hilo_v,
    gu_v,
    down_v,
    act_v,
    x_v,
    p_v,
    r_v,
    fin_v,
    inv_v,
    local_sem,
    p1_send,
    p1_recv,
    move_send,
    move_recv,
    own_send,
    own_recv,
    fin_recv,
):
    dev = lax.axis_index("expert")
    m = dev // flight
    e = dev % flight
    last = SPLIT - 1
    rows, width = hidden_v.shape
    experts = router_v.shape[1]
    slice_width = down_v.shape[0]
    cols = flight * CAP
    half = cols // 2
    part = half // 2
    place_q = (m, last - m)
    beyond = (dev + flight, dev - flight)

    def get_hidden(i):
        at = pl.ds(i * (width // PARTS), width // PARTS)
        return pltpu.make_async_copy(hidden_hbm.at[:, at], hidden_v.at[:, at], local_sem.at[4 + i])

    get_router = pltpu.make_async_copy(router_hbm, router_v, local_sem.at[0])
    weights = [
        pltpu.make_async_copy(gate_hbm.at[0], gu_v.at[:, pl.ds(0, slice_width)], local_sem.at[1]),
        pltpu.make_async_copy(
            up_hbm.at[0], gu_v.at[:, pl.ds(slice_width, slice_width)], local_sem.at[2]
        ),
        pltpu.make_async_copy(down_hbm.at[0], down_v, local_sem.at[3]),
    ]
    for i in range(PARTS):
        get_hidden(i).start()

    barrier = pltpu.get_barrier_semaphore()

    def greet(target):
        pl.semaphore_signal(barrier, inc=1, device_id={"expert": target}, device_id_type=MESH)

    @pl.loop(1, flight)
    def _(j):
        greet(m * flight + partner(e, j, flight))

    @pl.loop(0, flight)
    def _(j):
        @pl.when(m > 0)
        def _():
            greet((m - 1) * flight + j)

        @pl.when(m < last)
        def _():
            greet((m + 1) * flight + j)

    def remote(src, dst, ssem, rsem, target):
        return pltpu.make_async_remote_copy(
            src_ref=src,
            dst_ref=dst,
            send_sem=ssem,
            recv_sem=rsem,
            device_id={"expert": target},
            device_id_type=MESH,
        )

    def band(j):
        if isinstance(j, int):
            return pl.ds(j * CAP, CAP)
        return pl.ds(pl.multiple_of(j * CAP, CAP), CAP)

    def side(h):
        if isinstance(h, int):
            return pl.ds(h * half, half)
        return pl.ds(pl.multiple_of(h * half, half), half)

    wide = width // 2

    def wide_cols(ch):
        return pl.ds(pl.multiple_of(ch * wide, wide), wide)

    narrow = width // CHUNKS

    final = width // ENDS

    def final_cols(c):
        if isinstance(c, int):
            return pl.ds(c * final, final)
        return pl.ds(pl.multiple_of(c * final, final), final)

    def narrow_cols(c):
        if isinstance(c, int):
            return pl.ds(c * narrow, narrow)
        return pl.ds(pl.multiple_of(c * narrow, narrow), narrow)

    ids = ids_ref[...]
    earlier = lax.broadcasted_iota(jnp.int32, (rows, rows), 0) < lax.broadcasted_iota(
        jnp.int32, (rows, rows), 1
    )
    earlier = jnp.where(earlier, 1.0, 0.0).astype(BF16)
    named = lax.broadcasted_iota(jnp.int32, (max(8, flight), rows), 0)
    named = jnp.where(named < flight, partner(e, named % flight, flight), -1)
    hits = jnp.zeros((max(8, flight), rows), F32)
    for k in range(ids.shape[0]):
        hits = jnp.where(ids[k : k + 1, :] == named, 1.0, hits)
    slot = jnp.dot(hits.astype(BF16), earlier, preferred_element_type=F32)
    row_place = lax.broadcasted_iota(jnp.int32, (CAP, rows), 0).astype(F32)
    dispatch = jnp.concatenate(
        [
            jnp.where((hits[j : j + 1, :] > 0.5) & (slot[j : j + 1, :] == row_place), 1.0, 0.0)
            for j in range(flight)
        ],
        axis=0,
    ).astype(BF16)

    gain = gain_ref[...].astype(F32)[None, :]

    squares = jnp.zeros((cols, 1), F32)
    for ch in range(PARTS):
        at = pl.ds(ch * (width // PARTS), width // PARTS)
        get_hidden(ch).wait()
        picked_rows = jnp.dot(dispatch, hidden_v[:, at], preferred_element_type=F32)
        squares = squares + jnp.sum(picked_rows * picked_rows, axis=-1, keepdims=True)
        out_v[:, at] = picked_rows.astype(BF16)
    get_router.start()
    for copy in weights:
        copy.start()
    inv_v[...] = jnp.broadcast_to(lax.rsqrt(squares / width + 1e-06), inv_v.shape)

    def normalised(j):
        return (out_v[band(j), :].astype(F32) * inv_v[band(j), :1] * gain).astype(BF16)

    x_v[m, pl.ds(0, CAP), :] = normalised(0)

    pl.semaphore_wait(
        barrier, flight - 1 + jnp.where(m > 0, flight, 0) + jnp.where(m < last, flight, 0)
    )

    def first(j, ch):
        return remote(
            out_v.at[band(j), wide_cols(ch)],
            x_v.at[m, band(j), wide_cols(ch)],
            p1_send.at[0],
            p1_recv.at[j, ch],
            m * flight + partner(e, j, flight),
        )

    def rows_move(d, k, c, s, h):
        at = pl.ds(pl.multiple_of(h * half + (c // 2) * part, part), part)
        here = x_v.at[s, at, wide_cols(c % 2)]
        return remote(here, here, move_send.at[d], move_recv.at[d, k, c], beyond[d])

    def sums_move(d, k, c, s, h):
        return remote(
            p_v.at[s, side(h), narrow_cols(c)],
            r_v.at[d, s, side(h), narrow_cols(c)],
            move_send.at[d],
            move_recv.at[d, k, c],
            beyond[d],
        )

    def gathered(h, c):
        begin = h * (flight // 2) + (c // 2) * (flight // 4)

        @pl.loop(begin, begin + flight // 4)
        def _(j):
            @pl.when(j > 0)
            def _():
                first(j, c % 2).wait_recv()

    def begin_own(c):
        gathered(0, c)
        for d in range(2):

            @pl.when(place_q[d] < last)
            def _():
                rows_move(d, 0, c, m, 0).start()

    def begin_band(j):
        out_v[band(j), :] = normalised(j)
        for ch in range(2):
            first(j, ch).start()

    if flight == PARTS:
        begin_own(0)

    @pl.loop(1, flight // 2)
    def _(j):
        begin_band(j)

    @pl.loop(1 if flight == PARTS else 0, PARTS)
    def _(c):
        begin_own(c)

    @pl.loop(0, flight // 2)
    def _(i):
        begin_band(flight - 1 - i)

    @pl.loop(0, rows // CAP)
    def _(i):
        widened = hidden_v[band(i), :].astype(F32)
        inv_rms = lax.rsqrt(jnp.mean(widened * widened, axis=-1, keepdims=True) + 1e-06)
        normed_v[band(i), :] = (widened * inv_rms * gain).astype(BF16)

    get_router.wait()
    logits = jnp.dot(normed_v[...], router_v[...], preferred_element_type=F32)
    shifted = jnp.exp(logits - jnp.max(logits, axis=-1, keepdims=True))
    probs = shifted / jnp.sum(shifted, axis=-1, keepdims=True)
    expert = lax.broadcasted_iota(jnp.int32, (experts, rows), 0)
    chosen = jnp.zeros((experts, rows), F32)
    for k in range(ids.shape[0]):
        chosen = jnp.where(ids[k : k + 1, :] == expert, 1.0, chosen)
    picked = probs * chosen.T
    share = picked / jnp.sum(picked, axis=-1, keepdims=True)
    of_col = partner(e, lax.broadcasted_iota(jnp.int32, (experts, cols), 1) // CAP, flight)
    spread = jnp.where(lax.broadcasted_iota(jnp.int32, (experts, cols), 0) == of_col, 1.0, 0.0)
    spread = spread.astype(BF16)
    share_hi = share.astype(BF16)
    share_lo = (share - share_hi.astype(F32)).astype(BF16)
    hi_of = jnp.dot(share_hi, spread, preferred_element_type=F32)
    lo_of = jnp.dot(share_lo, spread, preferred_element_type=F32)
    same = lax.broadcasted_iota(jnp.int32, (rows, rows), 0) == lax.broadcasted_iota(
        jnp.int32, (rows, rows), 1
    )
    select = lax.dot_general(
        jnp.where(same, 1.0, 0.0).astype(BF16),
        dispatch,
        (((1,), (1,)), ((), ())),
        preferred_element_type=F32,
    )
    hilo_v[...] = jnp.concatenate(
        [jnp.where(select > 0.5, hi_of, 0.0), jnp.where(select > 0.5, lo_of, 0.0)], axis=1
    ).astype(BF16)

    def own_move(j):
        return remote(
            p_v.at[m, band(j)],
            fin_v.at[2, band(j)],
            own_send.at[0],
            own_recv.at[0],
            m * flight + partner(e, j, flight),
        )

    def final_move(d, c, j, h):
        there = m + 1 if d == 0 else m - 1
        return remote(
            p_v.at[there, band(j), final_cols(c)],
            fin_v.at[d, band(j), final_cols(c)],
            move_send.at[d],
            fin_recv.at[d, h, c],
            there * flight + partner(e, j, flight),
        )

    def send_sum(d, k, c, s, block, h):
        @pl.when(block == place_q[d] + 1)
        def _():
            @pl.loop(0, flight // 2)
            def _(i):
                even = flight // 4
                j = h * (flight // 2) + jnp.where(i < even, 2 * i + 1, 2 * (i - even))

                @pl.loop(c * (ENDS // CHUNKS), (c + 1) * (ENDS // CHUNKS))
                def _(end_c):
                    final_move(d, end_c, j, h).start()

        @pl.when(block > place_q[d] + 1)
        def _():
            sums_move(d, k, c, s, h).start()

    def in_pass(d, k):
        q = place_q[d]
        _, block, h = sent_in(q - 1, k - 1)
        s = block if d == 0 else last - block
        return s, h

    farther = jnp.where(place_q[0] > place_q[1], place_q[0], place_q[1])
    nearer = last - farther

    def combine(c):
        at = final_cols(c)
        for d in range(2):

            @pl.when(place_q[d] > 0)
            def _():
                for h in range(2):
                    here = fin_v.at[d, side(h), at]
                    remote(here, here, move_send.at[d], fin_recv.at[d, h, c], dev).wait_recv()

        total = fin_v[2, :, at].astype(F32)
        above = fin_v[jnp.where(m < last, 1, 0), :, at].astype(F32)
        below = fin_v[jnp.where(m > 0, 0, 1), :, at].astype(F32)
        both = jnp.where((m > 0) & (m < last), 1.0, 0.0)
        results = (total + above + both * below).astype(BF16)
        moe_ref[:, at] = jnp.dot(
            hilo_v[...], jnp.concatenate([results, results], axis=0), preferred_element_type=F32
        ).astype(BF16)

    def sums(k, c, coming, begun, bh):
        at = narrow_cols(c)
        for d in range(2):
            q = place_q[d]
            _, is_sum, block, h, s = coming[d]

            @pl.when(is_sum)
            def _():
                sums_move(d, k, c, s, h).wait_recv()
                p_v[s, side(h), at] = (
                    p_v[s, side(h), at].astype(F32) + r_v[d, s, side(h), at].astype(F32)
                ).astype(BF16)
                send_sum(d, k + 1, c, s, block, h)

            @pl.when((q == 0) & (k > 0))
            def _():
                send_sum(d, k + 1, c, begun if d == 0 else last - begun, begun, bh)

    @pl.loop(0, SLOTS - 1)
    def _(k):
        @pl.when(k == 1)
        def _():
            for copy in weights:
                copy.wait()

        @pl.when((k > 0) & (k <= 2 * farther))
        def _():
            s0, h0 = in_pass(0, k)
            s1, h1 = in_pass(1, k)
            up_far = place_q[0] > place_q[1]
            sf, hf = jnp.where(up_far, s0, s1), jnp.where(up_far, h0, h1)
            sn, hn = jnp.where(up_far, s1, s0), jnp.where(up_far, h1, h0)
            own = (k == 2 * nearer + 1) | (k == 2 * nearer + 2)
            s0, h0 = sf, hf
            s1 = jnp.where(k <= 2 * nearer, sn, jnp.where(own, m, sf))
            h1 = jnp.where(k <= 2 * nearer, hn, jnp.where(own, k - 2 * nearer - 1, hf))
            both = jnp.concatenate([x_v[s0, side(h0), :], x_v[s1, side(h1), :]], axis=0)
            gu = jnp.dot(both, gu_v[...], preferred_element_type=F32)
            act_v[...] = (jax.nn.silu(gu[:, :slice_width]) * gu[:, slice_width:]).astype(BF16)

            @pl.loop(0, PARTS)
            def _(i):
                at = pl.ds(pl.multiple_of(i * (width // PARTS), width // PARTS), width // PARTS)
                product = jnp.dot(
                    act_v[...], down_v[:, at], preferred_element_type=F32
                ).astype(BF16)
                p_v[s0, side(h0), at] = product[:half, :]
                p_v[s1, side(h1), at] = product[half:, :]

        for h in range(2):

            @pl.when(k == 2 * nearer + 1 + h)
            def _():
                if h == 0:
                    fin_v[2, band(0), :] = p_v[m, band(0), :]
                for j in range(max(1, h * (flight // 2)), (h + 1) * (flight // 2)):
                    own_move(j).start()

        coming = []
        for d in range(2):
            q = place_q[d]
            rows_in, block, h = sent_in(q - 1, k)
            is_rows = (q > 0) & rows_in
            is_sum = (q > 0) & jnp.logical_not(rows_in) & (block > q)
            coming.append((is_rows, is_sum, block, h, block if d == 0 else last - block))
        _, begun, bh = sent_in(0, k + 1)

        @pl.loop(0, PARTS)
        def _(part_c):
            @pl.when(k == 0)
            def _():
                gathered(1, part_c)

            for d in range(2):
                q = place_q[d]
                is_rows, _, _, h, s = coming[d]

                @pl.when(is_rows)
                def _():
                    rows_move(d, k, part_c, s, h).wait_recv()

                    @pl.when(q < last)
                    def _():
                        rows_move(d, k + 1, part_c, s, h).start()

                @pl.when((k == 2 * q) & (q < last))
                def _():
                    rows_move(d, k + 1, part_c, m, 1).start()

            @pl.when(part_c % (PARTS // CHUNKS) == PARTS // CHUNKS - 1)
            def _():
                c = part_c // (PARTS // CHUNKS)
                sums(k, c, coming, begun, bh)

    others = pl.ds(CAP, cols - CAP)
    remote(
        fin_v.at[2, others], fin_v.at[2, others], own_send.at[0], own_recv.at[0], dev
    ).wait_recv()
    for c in range(ENDS):
        combine(c)

    remote(out_v.at[others], out_v.at[others], p1_send.at[0], p1_recv.at[0, 0], dev).wait_send()
    remote(p_v.at[m, others], p_v.at[m, others], own_send.at[0], own_recv.at[0], dev).wait_send()
    for d in range(2):

        @pl.when(place_q[d] < last)
        def _():
            remote(x_v, x_v, move_send.at[d], move_recv.at[d, 0, 0], dev).wait_send()


def shards(flight, hidden, norm_gain, router_weight, expert_ids, gate_weight, up_weight, down_weight):
    rows, width = hidden.shape
    experts = router_weight.shape[1]
    cols = flight * CAP
    slice_width = gate_weight.shape[2]
    vmem = pl.BlockSpec(memory_space=pltpu.VMEM)
    hbm = pl.BlockSpec(memory_space=pltpu.HBM)
    dma = pltpu.SemaphoreType.DMA
    blocks = 2 * width * (16 * cols + 4 * cols + 3 * rows + experts + 3 * slice_width)
    grant = max(105 * 2**19, blocks + 2**23)
    return pl.pallas_call(
        functools.partial(kernel, flight),
        out_shape=jax.ShapeDtypeStruct((rows, width), BF16),
        in_specs=[vmem] * 2 + [hbm] * 5,
        out_specs=vmem,
        scratch_shapes=[
            pltpu.VMEM((rows, width), BF16),
            pltpu.VMEM((width, experts), BF16),
            pltpu.VMEM((rows, width), BF16),
            pltpu.VMEM((cols, width), BF16),
            pltpu.VMEM((rows, 2 * cols), BF16),
            pltpu.VMEM((width, 2 * slice_width), BF16),
            pltpu.VMEM((slice_width, width), BF16),
            pltpu.VMEM((cols, slice_width), BF16),
            pltpu.VMEM((SPLIT, cols, width), BF16),
            pltpu.VMEM((SPLIT, cols, width), BF16),
            pltpu.VMEM((2, SPLIT, cols, width), BF16),
            pltpu.VMEM((3, cols, width), BF16),
            pltpu.VMEM((cols, 128), F32),
            dma((4 + PARTS,)),
            dma((1,)),
            dma((flight, 2)),
            dma((2,)),
            dma((2, SLOTS, max(PARTS, CHUNKS))),
            dma((1,)),
            dma((1,)),
            dma((2, 2, ENDS)),
        ],
        compiler_params=pltpu.CompilerParams(
            collective_id=0, has_side_effects=True, vmem_limit_bytes=grant
        ),
    )(norm_gain, expert_ids.T, hidden, router_weight, gate_weight, up_weight, down_weight)


def solution(mesh):
    flight = mesh.shape["expert"] // SPLIT
    in_specs = (
        P(("group", "expert"), None),
        P(),
        P(),
        P(("group", "expert"), None),
        P("expert", None, None),
        P("expert", None, None),
        P("expert", None, None),
    )
    out_specs = P(("group", "expert"), None)
    return jax.shard_map(
        functools.partial(shards, flight),
        mesh=mesh,
        in_specs=in_specs,
        out_specs=out_specs,
        check_vma=False,
    )
```

```python
import functools

import jax
import jax.numpy as jnp
from jax import lax
from jax.experimental import pallas as pl
from jax.experimental.pallas import tpu as pltpu
from jax.sharding import PartitionSpec as P

SPLIT = 4
CAP = 16
SLOTS = 2 * SPLIT
PARTS = 4
CHUNKS = 2
ENDS = 4
F32 = jnp.float32
BF16 = jnp.bfloat16
MESH = pl.DeviceIdType.MESH


def exclusive(e, j, flight):
    total, bit = 0, 1
    while bit < flight:
        total = total + bit * ((e // bit + j // bit) % 2)
        bit *= 2
    return total


def partner(e, p, flight):
    return exclusive(e, p // 2 + (p % 2) * (flight // 2), flight)


def sent_in(q, k):
    last = SPLIT - 1
    rows = k < 2 * (q + 1)
    r = k - 2 * (q + 1)
    n = last - q
    block = jnp.where(
        rows, jnp.where(k <= q, q - k, k - q - 1), jnp.where(r < n, q + 1 + r, last - (r - n))
    )
    half = jnp.where(rows, jnp.where(k <= q, 0, 1), jnp.where(r < n, 0, 1))
    return rows, block, half


def kernel(
    flight,
    gain_ref,
    ids_ref,
    hidden_hbm,
    router_hbm,
    gate_hbm,
    up_hbm,
    down_hbm,
    moe_ref,
    hidden_v,
    router_v,
    normed_v,
    out_v,
    hilo_v,
    gu_v,
    down_v,
    act_v,
    x_v,
    p_v,
    r_v,
    fin_v,
    inv_v,
    local_sem,
    p1_send,
    p1_recv,
    move_send,
    move_recv,
    own_send,
    own_recv,
    fin_recv,
):
    dev = lax.axis_index("expert")
    m = dev // flight
    e = dev % flight
    last = SPLIT - 1
    rows, width = hidden_v.shape
    experts = router_v.shape[1]
    slice_width = down_v.shape[0]
    cols = flight * CAP
    half = cols // 2
    part = half // 2
    place_q = (m, last - m)
    beyond = (dev + flight, dev - flight)

    def get_hidden(i):
        at = pl.ds(i * (width // PARTS), width // PARTS)
        return pltpu.make_async_copy(hidden_hbm.at[:, at], hidden_v.at[:, at], local_sem.at[4 + i])

    get_router = pltpu.make_async_copy(router_hbm, router_v, local_sem.at[0])
    weights = [
        pltpu.make_async_copy(gate_hbm.at[0], gu_v.at[:, pl.ds(0, slice_width)], local_sem.at[1]),
        pltpu.make_async_copy(
            up_hbm.at[0], gu_v.at[:, pl.ds(slice_width, slice_width)], local_sem.at[2]
        ),
        pltpu.make_async_copy(down_hbm.at[0], down_v, local_sem.at[3]),
    ]
    for i in range(PARTS):
        get_hidden(i).start()

    barrier = pltpu.get_barrier_semaphore()

    def greet(target):
        pl.semaphore_signal(barrier, inc=1, device_id={"expert": target}, device_id_type=MESH)

    @pl.loop(1, flight)
    def _(j):
        greet(m * flight + partner(e, j, flight))

    @pl.loop(0, flight)
    def _(j):
        @pl.when(m > 0)
        def _():
            greet((m - 1) * flight + j)

        @pl.when(m < last)
        def _():
            greet((m + 1) * flight + j)

    def remote(src, dst, ssem, rsem, target):
        return pltpu.make_async_remote_copy(
            src_ref=src,
            dst_ref=dst,
            send_sem=ssem,
            recv_sem=rsem,
            device_id={"expert": target},
            device_id_type=MESH,
        )

    def band(j):
        if isinstance(j, int):
            return pl.ds(j * CAP, CAP)
        return pl.ds(pl.multiple_of(j * CAP, CAP), CAP)

    def side(h):
        if isinstance(h, int):
            return pl.ds(h * half, half)
        return pl.ds(pl.multiple_of(h * half, half), half)

    wide = width // 2

    def wide_cols(ch):
        return pl.ds(pl.multiple_of(ch * wide, wide), wide)

    narrow = width // CHUNKS

    final = width // ENDS

    def final_cols(c):
        if isinstance(c, int):
            return pl.ds(c * final, final)
        return pl.ds(pl.multiple_of(c * final, final), final)

    def narrow_cols(c):
        if isinstance(c, int):
            return pl.ds(c * narrow, narrow)
        return pl.ds(pl.multiple_of(c * narrow, narrow), narrow)

    ids = ids_ref[...]
    earlier = lax.broadcasted_iota(jnp.int32, (rows, rows), 0) < lax.broadcasted_iota(
        jnp.int32, (rows, rows), 1
    )
    earlier = jnp.where(earlier, 1.0, 0.0).astype(BF16)
    named = lax.broadcasted_iota(jnp.int32, (max(8, flight), rows), 0)
    named = jnp.where(named < flight, partner(e, named % flight, flight), -1)
    hits = jnp.zeros((max(8, flight), rows), F32)
    for k in range(ids.shape[0]):
        hits = jnp.where(ids[k : k + 1, :] == named, 1.0, hits)
    slot = jnp.dot(hits.astype(BF16), earlier, preferred_element_type=F32)
    row_place = lax.broadcasted_iota(jnp.int32, (CAP, rows), 0).astype(F32)
    dispatch = jnp.concatenate(
        [
            jnp.where((hits[j : j + 1, :] > 0.5) & (slot[j : j + 1, :] == row_place), 1.0, 0.0)
            for j in range(flight)
        ],
        axis=0,
    ).astype(BF16)

    gain = gain_ref[...].astype(F32)[None, :]

    squares = jnp.zeros((cols, 1), F32)
    for ch in range(PARTS):
        at = pl.ds(ch * (width // PARTS), width // PARTS)
        get_hidden(ch).wait()
        picked_rows = jnp.dot(dispatch, hidden_v[:, at], preferred_element_type=F32)
        squares = squares + jnp.sum(picked_rows * picked_rows, axis=-1, keepdims=True)
        out_v[:, at] = picked_rows.astype(BF16)
    get_router.start()
    for copy in weights:
        copy.start()
    inv_v[...] = jnp.broadcast_to(lax.rsqrt(squares / width + 1e-06), inv_v.shape)

    def normalised(j):
        return (out_v[band(j), :].astype(F32) * inv_v[band(j), :1] * gain).astype(BF16)

    x_v[m, pl.ds(0, CAP), :] = normalised(0)

    pl.semaphore_wait(
        barrier, flight - 1 + jnp.where(m > 0, flight, 0) + jnp.where(m < last, flight, 0)
    )

    def first(j, ch):
        return remote(
            out_v.at[band(j), wide_cols(ch)],
            x_v.at[m, band(j), wide_cols(ch)],
            p1_send.at[0],
            p1_recv.at[j, ch],
            m * flight + partner(e, j, flight),
        )

    def rows_move(d, k, c, s, h):
        at = pl.ds(pl.multiple_of(h * half + (c // 2) * part, part), part)
        here = x_v.at[s, at, wide_cols(c % 2)]
        return remote(here, here, move_send.at[d], move_recv.at[d, k, c], beyond[d])

    def sums_move(d, k, c, s, h):
        return remote(
            p_v.at[s, side(h), narrow_cols(c)],
            r_v.at[d, s, side(h), narrow_cols(c)],
            move_send.at[d],
            move_recv.at[d, k, c],
            beyond[d],
        )

    def gathered(h, c):
        begin = h * (flight // 2) + (c // 2) * (flight // 4)

        @pl.loop(begin, begin + flight // 4)
        def _(j):
            @pl.when(j > 0)
            def _():
                first(j, c % 2).wait_recv()

    def begin_own(c):
        gathered(0, c)
        for d in range(2):

            @pl.when(place_q[d] < last)
            def _():
                rows_move(d, 0, c, m, 0).start()

    def begin_band(j):
        out_v[band(j), :] = normalised(j)
        for ch in range(2):
            first(j, ch).start()

    if flight == PARTS:
        begin_own(0)

    @pl.loop(1, flight // 2)
    def _(j):
        begin_band(j)

    @pl.loop(1 if flight == PARTS else 0, PARTS)
    def _(c):
        begin_own(c)

    @pl.loop(0, flight // 2)
    def _(i):
        begin_band(flight - 1 - i)

    @pl.loop(0, rows // CAP)
    def _(i):
        widened = hidden_v[band(i), :].astype(F32)
        inv_rms = lax.rsqrt(jnp.mean(widened * widened, axis=-1, keepdims=True) + 1e-06)
        normed_v[band(i), :] = (widened * inv_rms * gain).astype(BF16)

    get_router.wait()
    logits = jnp.dot(normed_v[...], router_v[...], preferred_element_type=F32)
    shifted = jnp.exp(logits - jnp.max(logits, axis=-1, keepdims=True))
    probs = shifted / jnp.sum(shifted, axis=-1, keepdims=True)
    expert = lax.broadcasted_iota(jnp.int32, (experts, rows), 0)
    chosen = jnp.zeros((experts, rows), F32)
    for k in range(ids.shape[0]):
        chosen = jnp.where(ids[k : k + 1, :] == expert, 1.0, chosen)
    picked = probs * chosen.T
    share = picked / jnp.sum(picked, axis=-1, keepdims=True)
    of_col = partner(e, lax.broadcasted_iota(jnp.int32, (experts, cols), 1) // CAP, flight)
    spread = jnp.where(lax.broadcasted_iota(jnp.int32, (experts, cols), 0) == of_col, 1.0, 0.0)
    spread = spread.astype(BF16)
    share_hi = share.astype(BF16)
    share_lo = (share - share_hi.astype(F32)).astype(BF16)
    hi_of = jnp.dot(share_hi, spread, preferred_element_type=F32)
    lo_of = jnp.dot(share_lo, spread, preferred_element_type=F32)
    same = lax.broadcasted_iota(jnp.int32, (rows, rows), 0) == lax.broadcasted_iota(
        jnp.int32, (rows, rows), 1
    )
    select = lax.dot_general(
        jnp.where(same, 1.0, 0.0).astype(BF16),
        dispatch,
        (((1,), (1,)), ((), ())),
        preferred_element_type=F32,
    )
    hilo_v[...] = jnp.concatenate(
        [jnp.where(select > 0.5, hi_of, 0.0), jnp.where(select > 0.5, lo_of, 0.0)], axis=1
    ).astype(BF16)

    def own_move(j):
        return remote(
            p_v.at[m, band(j)],
            fin_v.at[2, band(j)],
            own_send.at[0],
            own_recv.at[0],
            m * flight + partner(e, j, flight),
        )

    def final_move(d, c, j, h):
        there = m + 1 if d == 0 else m - 1
        return remote(
            p_v.at[there, band(j), final_cols(c)],
            fin_v.at[d, band(j), final_cols(c)],
            move_send.at[d],
            fin_recv.at[d, h, c],
            there * flight + partner(e, j, flight),
        )

    def send_sum(d, k, c, s, block, h):
        @pl.when(block == place_q[d] + 1)
        def _():
            @pl.loop(0, flight // 2)
            def _(i):
                even = flight // 4
                j = h * (flight // 2) + jnp.where(i < even, 2 * i + 1, 2 * (i - even))

                @pl.loop(c * (ENDS // CHUNKS), (c + 1) * (ENDS // CHUNKS))
                def _(end_c):
                    final_move(d, end_c, j, h).start()

        @pl.when(block > place_q[d] + 1)
        def _():
            sums_move(d, k, c, s, h).start()

    def in_pass(d, k):
        q = place_q[d]
        _, block, h = sent_in(q - 1, k - 1)
        s = block if d == 0 else last - block
        return s, h

    farther = jnp.where(place_q[0] > place_q[1], place_q[0], place_q[1])
    nearer = last - farther

    def combine(c):
        at = final_cols(c)
        for d in range(2):

            @pl.when(place_q[d] > 0)
            def _():
                for h in range(2):
                    here = fin_v.at[d, side(h), at]
                    remote(here, here, move_send.at[d], fin_recv.at[d, h, c], dev).wait_recv()

        total = fin_v[2, :, at].astype(F32)
        above = fin_v[jnp.where(m < last, 1, 0), :, at].astype(F32)
        below = fin_v[jnp.where(m > 0, 0, 1), :, at].astype(F32)
        both = jnp.where((m > 0) & (m < last), 1.0, 0.0)
        results = (total + above + both * below).astype(BF16)
        moe_ref[:, at] = jnp.dot(
            hilo_v[...], jnp.concatenate([results, results], axis=0), preferred_element_type=F32
        ).astype(BF16)

    def sums(k, c, coming, begun, bh):
        at = narrow_cols(c)
        for d in range(2):
            q = place_q[d]
            _, is_sum, block, h, s = coming[d]

            @pl.when(is_sum)
            def _():
                sums_move(d, k, c, s, h).wait_recv()
                p_v[s, side(h), at] = (
                    p_v[s, side(h), at].astype(F32) + r_v[d, s, side(h), at].astype(F32)
                ).astype(BF16)
                send_sum(d, k + 1, c, s, block, h)

            @pl.when((q == 0) & (k > 0))
            def _():
                send_sum(d, k + 1, c, begun if d == 0 else last - begun, begun, bh)

    @pl.loop(0, SLOTS - 1)
    def _(k):
        @pl.when(k == 1)
        def _():
            for copy in weights:
                copy.wait()

        @pl.when((k > 0) & (k <= 2 * farther))
        def _():
            s0, h0 = in_pass(0, k)
            s1, h1 = in_pass(1, k)
            up_far = place_q[0] > place_q[1]
            sf, hf = jnp.where(up_far, s0, s1), jnp.where(up_far, h0, h1)
            sn, hn = jnp.where(up_far, s1, s0), jnp.where(up_far, h1, h0)
            own = (k == 2 * nearer + 1) | (k == 2 * nearer + 2)
            s0, h0 = sf, hf
            s1 = jnp.where(k <= 2 * nearer, sn, jnp.where(own, m, sf))
            h1 = jnp.where(k <= 2 * nearer, hn, jnp.where(own, k - 2 * nearer - 1, hf))
            both = jnp.concatenate([x_v[s0, side(h0), :], x_v[s1, side(h1), :]], axis=0)
            gu = jnp.dot(both, gu_v[...], preferred_element_type=F32)
            act_v[...] = (jax.nn.silu(gu[:, :slice_width]) * gu[:, slice_width:]).astype(BF16)

            @pl.loop(0, PARTS)
            def _(i):
                at = pl.ds(pl.multiple_of(i * (width // PARTS), width // PARTS), width // PARTS)
                product = jnp.dot(
                    act_v[...], down_v[:, at], preferred_element_type=F32
                ).astype(BF16)
                p_v[s0, side(h0), at] = product[:half, :]
                p_v[s1, side(h1), at] = product[half:, :]

        coming = []
        for d in range(2):
            q = place_q[d]
            rows_in, block, h = sent_in(q - 1, k)
            is_rows = (q > 0) & rows_in
            is_sum = (q > 0) & jnp.logical_not(rows_in) & (block > q)
            coming.append((is_rows, is_sum, block, h, block if d == 0 else last - block))
        _, begun, bh = sent_in(0, k + 1)

        @pl.loop(0, PARTS)
        def _(part_c):
            @pl.when(k == 0)
            def _():
                gathered(1, part_c)

            for d in range(2):
                q = place_q[d]
                is_rows, _, _, h, s = coming[d]

                @pl.when(is_rows)
                def _():
                    rows_move(d, k, part_c, s, h).wait_recv()

                    @pl.when(q < last)
                    def _():
                        rows_move(d, k + 1, part_c, s, h).start()

                @pl.when((k == 2 * q) & (q < last))
                def _():
                    rows_move(d, k + 1, part_c, m, 1).start()

            @pl.when(part_c % (PARTS // CHUNKS) == PARTS // CHUNKS - 1)
            def _():
                c = part_c // (PARTS // CHUNKS)
                sums(k, c, coming, begun, bh)

        for h in range(2):

            @pl.when(k == 2 * nearer + 1 + h)
            def _():
                if h == 0:
                    fin_v[2, band(0), :] = p_v[m, band(0), :]
                for j in range(max(1, h * (flight // 2)), (h + 1) * (flight // 2)):
                    own_move(j).start()

    others = pl.ds(CAP, cols - CAP)
    remote(
        fin_v.at[2, others], fin_v.at[2, others], own_send.at[0], own_recv.at[0], dev
    ).wait_recv()
    for c in range(ENDS):
        combine(c)

    remote(out_v.at[others], out_v.at[others], p1_send.at[0], p1_recv.at[0, 0], dev).wait_send()
    remote(p_v.at[m, others], p_v.at[m, others], own_send.at[0], own_recv.at[0], dev).wait_send()
    for d in range(2):

        @pl.when(place_q[d] < last)
        def _():
            remote(x_v, x_v, move_send.at[d], move_recv.at[d, 0, 0], dev).wait_send()


def shards(flight, hidden, norm_gain, router_weight, expert_ids, gate_weight, up_weight, down_weight):
    rows, width = hidden.shape
    experts = router_weight.shape[1]
    cols = flight * CAP
    slice_width = gate_weight.shape[2]
    vmem = pl.BlockSpec(memory_space=pltpu.VMEM)
    hbm = pl.BlockSpec(memory_space=pltpu.HBM)
    dma = pltpu.SemaphoreType.DMA
    blocks = 2 * width * (16 * cols + 4 * cols + 3 * rows + experts + 3 * slice_width)
    grant = max(105 * 2**19, blocks + 2**23)
    return pl.pallas_call(
        functools.partial(kernel, flight),
        out_shape=jax.ShapeDtypeStruct((rows, width), BF16),
        in_specs=[vmem] * 2 + [hbm] * 5,
        out_specs=vmem,
        scratch_shapes=[
            pltpu.VMEM((rows, width), BF16),
            pltpu.VMEM((width, experts), BF16),
            pltpu.VMEM((rows, width), BF16),
            pltpu.VMEM((cols, width), BF16),
            pltpu.VMEM((rows, 2 * cols), BF16),
            pltpu.VMEM((width, 2 * slice_width), BF16),
            pltpu.VMEM((slice_width, width), BF16),
            pltpu.VMEM((cols, slice_width), BF16),
            pltpu.VMEM((SPLIT, cols, width), BF16),
            pltpu.VMEM((SPLIT, cols, width), BF16),
            pltpu.VMEM((2, SPLIT, cols, width), BF16),
            pltpu.VMEM((3, cols, width), BF16),
            pltpu.VMEM((cols, 128), F32),
            dma((4 + PARTS,)),
            dma((1,)),
            dma((flight, 2)),
            dma((2,)),
            dma((2, SLOTS, max(PARTS, CHUNKS))),
            dma((1,)),
            dma((1,)),
            dma((2, 2, ENDS)),
        ],
        compiler_params=pltpu.CompilerParams(
            collective_id=0, has_side_effects=True, vmem_limit_bytes=grant
        ),
    )(norm_gain, expert_ids.T, hidden, router_weight, gate_weight, up_weight, down_weight)


def solution(mesh):
    flight = mesh.shape["expert"] // SPLIT
    in_specs = (
        P(("group", "expert"), None),
        P(),
        P(),
        P(("group", "expert"), None),
        P("expert", None, None),
        P("expert", None, None),
        P("expert", None, None),
    )
    out_specs = P(("group", "expert"), None)
    return jax.shard_map(
        functools.partial(shards, flight),
        mesh=mesh,
        in_specs=in_specs,
        out_specs=out_specs,
        check_vma=False,
    )
```
